32 devices in a mesh: gx: 4 (over y, x), gy: 4 (over z), gz: 2 (over core).
Axes of the slice: x: 2, y: 2, z: 4, core: 2. Of those that a mesh axis runs over, the one named last changes fastest.
Arguments:
- positions: float32 [2048, 3, 128], P(('gx', 'gy', 'gz')), may hold values from 0 to 1
- charges: float32 [2048, 128], P(('gx', 'gy', 'gz')), may hold values from -0.18 to 0.18
- counts: int32 [2048], P(('gx', 'gy', 'gz')), may hold values from 1 to 128
- up_inverse: float32 [64, 64], replicated, may hold values from -0.09375 to 0.09375
- down_inverse: float32 [64, 64], replicated, may hold values from -0.09375 to 0.09375
- inner_surface: float32 [3, 64], replicated, may hold values from 0.15 to 0.85
- outer_surface: float32 [3, 64], replicated, may hold values from -1 to 2, as said below
Outputs:
- potential: float32 [2048, 128], P(('gx', 'gy', 'gz'))
The draws below stay inside these ranges and needn't reach their ends.
Inputs may be any that keep to these rules, and one draw needn't show every extreme that they name: `outer_surface`: each point lies on the boundary of the cube [-1, 2]^3.
All inputs are finite; a program needn't handle non-finite values.
Results may differ from the reference program's by a relative error of at most 0.0003.
Values sent between devices are 32-bit elements; how exact they have to be, the bound alone decides.
A program may use at most 64 MiB of HBM per device.

```python
from functools import partial
import jax
import jax.numpy as jnp
import numpy as np
from jax import lax

CX = 4
CY = 4
CZ = 4
PTS = 128
TERMS = 64
LEAVES = 2048
DEVICES = 32


def draw_outer_surface(key, part):
    first_key, second_key, third_key = jax.random.split(jax.random.fold_in(key, 7), 3)
    spot = jax.random.uniform(first_key, (3, TERMS), jnp.float32, -1.0, 1.0)
    facing = jax.random.randint(second_key, (TERMS,), 0, 3)
    signed = jax.random.randint(third_key, (TERMS,), 0, 2).astype(jnp.float32) * 2.0 - 1.0
    picked = jnp.arange(3)[:, None] == facing[None, :]
    cube = jnp.where(picked, signed[None, :], spot)
    return 0.5 + 1.5 * cube


def set_ends(array, key, least, top_value):
    dims = array.shape
    place = [jax.random.randint(jax.random.fold_in(key, axis), (), 0, dims[axis]) for axis in range(len(dims))]
    array = array.at[tuple(place)].set(least)
    longest = dims.index(max(dims))
    place[longest] = (place[longest] + 1) % dims[longest]
    return array.at[tuple(place)].set(top_value)


def shard_levels(rng, shape, pieces, low, high):
    gain = 1.0
    for axis_at, blocks in pieces:
        heights = jax.random.uniform(jax.random.fold_in(jax.random.fold_in(rng, 6), axis_at), (blocks,), jnp.float32, low / len(pieces), high / len(pieces))
        gain = gain * jnp.repeat(jnp.exp(heights), shape[axis_at] // blocks).reshape((-1,) + (1,) * (len(shape) - 1 - axis_at))
    return gain


def noise(own_key, shape, scale, limit, cuts=(), kind=jnp.bfloat16):
    drawn = jax.random.normal(own_key, shape, jnp.float32) * scale
    if len(cuts) > 0:
        drawn = shard_levels(own_key, shape, cuts, -0.22, 0.18) * drawn
    return jnp.clip(drawn, min=-limit, max=limit).astype(kind)


def setup_inputs(seed: int = 0) -> dict:
    key_list = jax.random.split(jax.random.key(seed), 8)
    return {
        "positions": jnp.clip(1.0 * jax.random.uniform(key_list[0], (LEAVES, 3, PTS), jnp.float32) ** shard_levels(key_list[0], (LEAVES, 3, PTS), ((0, 32),), -0.2, 0.2), 0.0, 1.0),
        "charges": noise(key_list[1], (LEAVES, PTS), 0.03, 0.18, ((0, 32),), jnp.float32),
        "counts": set_ends(jax.random.randint(key_list[2], (LEAVES,), 1, PTS + 1), jax.random.fold_in(key_list[2], 1), 1, PTS).astype(jnp.int32),
        "up_inverse": noise(key_list[3], (TERMS, TERMS), (TERMS * TERMS) ** -0.5, 0.09375, (), jnp.float32),
        "down_inverse": noise(key_list[4], (TERMS, TERMS), (TERMS * TERMS) ** -0.5, 0.09375, (), jnp.float32),
        "inner_surface": jnp.clip(jax.random.uniform(key_list[5], (3, TERMS), jnp.float32, 0.15, 0.85), 0.15, 0.85),
        "outer_surface": draw_outer_surface(jax.random.fold_in(key_list[7], 71), 0),
    }


SOFTEN = 0.0025
EXACT_DOTS = lax.Precision.HIGHEST

def kernel(square):
    return 1.0 / jnp.sqrt(square + SOFTEN)

def leaf_blocks(function, arrays, block_size):
    leaf_count = arrays[0].shape[0]
    shaped = tuple((member.reshape((leaf_count // block_size, block_size) + member.shape[1:]) for member in arrays))
    result = lax.map(lambda members: function(*members), shaped)
    return result.reshape((leaf_count,) + result.shape[2:])

def upward(outer, position, charge):
    square = jnp.zeros((position.shape[0], outer.shape[1], position.shape[2]), jnp.float32)
    for dimension in range(3):
        spread = outer[dimension][None, :, None] - position[:, dimension, None, :]
        square = square + spread * spread
    return jnp.einsum('nij,nj->ni', kernel(square), charge, precision=EXACT_DOTS)

def downward(outer, position, weight):
    square = jnp.zeros((position.shape[0], position.shape[2], outer.shape[1]), jnp.float32)
    for dimension in range(3):
        spread = position[:, dimension, :, None] - outer[dimension][None, None, :]
        square = square + spread * spread
    return jnp.einsum('nti,ni->nt', kernel(square), weight, precision=EXACT_DOTS)

def pair_potential(target, source, shift, exclude):
    square = jnp.zeros((target.shape[0], target.shape[2], source.shape[2]), jnp.float32)
    for dimension in range(3):
        spread = target[:, dimension, :, None] - source[:, dimension, None, :] - shift[dimension]
        square = square + spread * spread
    weight = kernel(square)
    if exclude:
        weight = weight * (1.0 - jnp.eye(target.shape[2], dtype=jnp.float32))
    return jnp.einsum('nts,ns->nt', weight, source[:, 3, :], precision=EXACT_DOTS)

def allowed(parity, shift):
    return jnp.abs(jnp.floor_divide(parity + shift, 2)) <= 1

def translate(extended, inner, span_x, span_y, span_z):
    parity_x = jnp.arange(span_x, dtype=jnp.int32) % 2
    parity_y = jnp.arange(span_y, dtype=jnp.int32) % 2
    parity_z = jnp.arange(span_z, dtype=jnp.int32) % 2
    shifts_z = jnp.arange(-3, 4, dtype=jnp.int32)
    terms_count = inner.shape[1]

    def over_x(accum, shift_x):
        slab = lax.dynamic_slice_in_dim(extended, shift_x + 3, span_x, axis=0)
        okay_x = allowed(parity_x, shift_x)
        okay_z = allowed(parity_z[None, :], shifts_z[:, None])
        spread_x = inner[0][:, None] - inner[0][None, :] - shift_x.astype(jnp.float32)
        spread_z = inner[2][None, :, None] - inner[2][None, None, :] - shifts_z.astype(jnp.float32)[:, None, None]
        for shift_y in range(-3, 4):
            rows = slab[:, 3 + shift_y:3 + shift_y + span_y]
            stacked = jnp.stack([rows[:, :, 3 + shift_z:3 + shift_z + span_z] for shift_z in range(-3, 4)])
            okay_y = allowed(parity_y, shift_y)
            spread_y = inner[1][:, None] - inner[1][None, :] - float(shift_y)
            square = (spread_x * spread_x + spread_y * spread_y)[None] + spread_z * spread_z
            matrices = kernel(square)
            extent = jnp.maximum(jnp.maximum(jnp.abs(shift_x), abs(shift_y)), jnp.abs(shifts_z))
            mask = okay_x[None, :, None, None] & okay_y[None, None, :, None] & okay_z[:, None, None, :] & (extent >= 2)[:, None, None, None]
            weighted = stacked * mask[..., None].astype(jnp.float32)
            accum = accum + jnp.einsum('oxyzj,oij->xyzi', weighted, matrices, precision=EXACT_DOTS)
        return (accum, None)
    start = jnp.zeros((span_x, span_y, span_z, terms_count), jnp.float32)
    result, _ = lax.scan(over_x, start, jnp.arange(-3, 4, dtype=jnp.int32))
    return result

def box_tables():
    total_bits = DEVICES.bit_length() - 1
    bit_counts = [len(range(dimension, total_bits, 3)) for dimension in range(3)]
    corners = np.zeros((DEVICES, 3), np.int32)
    for device in range(DEVICES):
        for dimension in range(3):
            corners[device, dimension] = sum(((device >> dimension + 3 * rank & 1) << rank for rank in range(bit_counts[dimension])))
    extent = [1 << bit_counts[dimension] for dimension in range(3)]
    device_table = np.zeros(extent, np.int32)
    device_table[corners[:, 0], corners[:, 1], corners[:, 2]] = np.arange(DEVICES, dtype=np.int32)
    return (corners, device_table, extent)

def to_grid(flat, device_table, extent):
    trailing = flat.shape[1:]
    blocks = flat.reshape((DEVICES, CX, CY, CZ) + trailing)[device_table]
    permuted = (0, 3, 1, 4, 2, 5) + tuple(range(6, 6 + len(trailing)))
    return blocks.transpose(permuted).reshape((extent[0] * CX, extent[1] * CY, extent[2] * CZ) + trailing)

def from_grid(grid, corners, extent):
    trailing = grid.shape[3:]
    shaped = grid.reshape((extent[0], CX, extent[1], CY, extent[2], CZ) + trailing)
    permuted = (0, 2, 4, 1, 3, 5) + tuple(range(6, 6 + len(trailing)))
    shaped = shaped.transpose(permuted)
    blocks = shaped[corners[:, 0], corners[:, 1], corners[:, 2]]
    return blocks.reshape((DEVICES * CX * CY * CZ,) + trailing)

def reference(positions, charges, counts, up_inverse, down_inverse, inner_surface, outer_surface):
    live = (jnp.arange(PTS, dtype=jnp.int32)[None, :] < counts[:, None]).astype(jnp.float32)
    source = charges * live
    check_up = leaf_blocks(partial(upward, outer_surface), (positions, source), 64)
    density = jnp.dot(check_up, up_inverse.T, preferred_element_type=jnp.float32, precision=EXACT_DOTS)
    corners, device_table, extent = box_tables()
    grid_x, grid_y, grid_z = (extent[0] * CX, extent[1] * CY, extent[2] * CZ)
    cell_total = grid_x * grid_y * grid_z
    dens_grid = to_grid(density, device_table, extent)
    point_grid = to_grid(jnp.concatenate([positions, source[:, None, :]], axis=1), device_table, extent)
    targets = point_grid[:, :, :, :3].reshape(cell_total, 3, PTS)
    padded = jnp.pad(point_grid, ((1, 1), (1, 1), (1, 1), (0, 0), (0, 0)))
    near = jnp.zeros((cell_total, PTS), jnp.float32)
    for shift_x in range(-1, 2):
        for shift_y in range(-1, 2):
            for shift_z in range(-1, 2):
                window = padded[1 + shift_x:1 + shift_x + grid_x, 1 + shift_y:1 + shift_y + grid_y, 1 + shift_z:1 + shift_z + grid_z]
                window = window.reshape(cell_total, 4, PTS)
                exclude = shift_x == 0 and shift_y == 0 and (shift_z == 0)
                near = near + leaf_blocks(partial(pair_potential, shift=(shift_x, shift_y, shift_z), exclude=exclude), (targets, window), 64)
    near = from_grid(near.reshape(grid_x, grid_y, grid_z, PTS), corners, extent)
    extended = jnp.pad(dens_grid, ((3, 3), (3, 3), (3, 3), (0, 0)))
    check_down = translate(extended, inner_surface, grid_x, grid_y, grid_z)
    check_down = from_grid(check_down, corners, extent)
    local = jnp.dot(check_down, down_inverse.T, preferred_element_type=jnp.float32, precision=EXACT_DOTS)
    far = leaf_blocks(partial(downward, outer_surface), (positions, local), 64)
    return live * (near + far)
```

```python
from functools import partial

import jax
import jax.numpy as jnp
from jax import lax
from jax.experimental import pallas as pl
from jax.experimental.pallas import tpu as pltpu
from jax.sharding import PartitionSpec as P

CX = 4
CY = 4
CZ = 4
PTS = 128
TERMS = 64
LEAF = CX * CY * CZ
EXT = (CX + 2) * (CY + 2) * (CZ + 2)
FEATS = 32
LINE = 4
PAIRS = 4


SOFTEN = 0.0025
EXACT_DOTS = lax.Precision.HIGHEST


def iota(shape, dimension):
    return lax.broadcasted_iota(jnp.int32, shape, dimension)


def column(row):
    size = row.shape[1]
    eye = iota((size, size), 0) == iota((size, size), 1)
    return jnp.sum(jnp.where(eye, row, 0.0), axis=1, keepdims=True)


def over_plane(size_x, size_y, body, start, unroll=1):
    def line(x, carry):
        return lax.fori_loop(0, size_y, lambda y, held: body(x, y, held), carry, unroll=unroll)

    return lax.fori_loop(0, size_x, line, start)


def rounded(value):
    return value.astype(jnp.bfloat16).astype(jnp.float32)


def three_parts(value):
    high = rounded(value)
    middle = rounded(value - high)
    low = rounded(value - high - middle)
    return high, middle, low


def squares_of(points, shift_x, shift_y, shift_z, extra):
    row = iota((8, PTS), 0) % 4
    twice = jnp.concatenate([points, points], axis=0)
    place = twice + jnp.where(row == 0, shift_x, jnp.where(row == 1, shift_y, shift_z))
    square = place * place
    norm = square[0:1] + square[1:2] + square[2:3] + extra
    return jnp.where(row == 3, norm, place), row == 3, iota((8, PTS), 0) < 4


def source_features(points, shift_x, shift_y, shift_z):
    value, last, first = squares_of(points, shift_x, shift_y, shift_z, 0.0)
    high, middle, low = three_parts(value)
    scale = jnp.where(last, 1.0, -2.0)
    high_one = jnp.where(last, 1.0, -2.0 * high)
    middle_one = jnp.where(last, 1.0, -2.0 * middle)
    rows = [
        jnp.where(first, high * scale, middle * scale),
        jnp.where(first, low * scale, high_one),
        jnp.where(first, high_one, middle_one),
        jnp.zeros((8, PTS), jnp.float32),
    ]
    return jnp.concatenate(rows, axis=0).astype(jnp.bfloat16)


def target_features(points, shift_x, shift_y, shift_z):
    value, last, first = squares_of(points, shift_x, shift_y, shift_z, SOFTEN)
    high, middle, low = three_parts(value)
    high_one = jnp.where(last, 1.0, high)
    rows = [
        high_one,
        jnp.where(first, high_one, jnp.where(last, high, middle)),
        jnp.where(first, jnp.where(last, middle, low), jnp.where(last, low, middle)),
        jnp.zeros((8, PTS), jnp.float32),
    ]
    return jnp.transpose(jnp.concatenate(rows, axis=0)).astype(jnp.bfloat16)


def whole():
    return pl.BlockSpec(memory_space=pltpu.VMEM)


def scalars():
    return pl.BlockSpec(memory_space=pltpu.SMEM)


def anywhere():
    return pl.BlockSpec(memory_space=pl.ANY)


def axis_bits():
    low_bits = lax.axis_size("gz").bit_length() - 1
    mid_bits = lax.axis_size("gy").bit_length() - 1
    high_bits = lax.axis_size("gx").bit_length() - 1
    return (low_bits, mid_bits, high_bits)


SIDES = [
    (x, y, z)
    for x in (-1, 0, 1)
    for y in (-1, 0, 1)
    for z in (-1, 0, 1)
    if (x, y, z) != (0, 0, 0)
]


def rim(side, size, layers):
    if side > 0:
        return pl.ds(size, layers), pl.ds(0, layers)
    if side < 0:
        return pl.ds(layers, layers), pl.ds(size + layers, layers)
    return pl.ds(layers, size), pl.ds(layers, size)


def middle(cell):
    if isinstance(cell, int):
        return jnp.float32(cell) - (CX // 2 + 1)
    return cell.astype(jnp.float32) - (CX // 2 + 1)


def ext_index(x, y, z):
    return ((x + 1) * (CY + 2) + y + 1) * (CZ + 2) + z + 1


def clear_part(grouped, surface):
    def one(n, carry):
        grouped[n] = jnp.zeros((8, 16, 2 * TERMS), jnp.bfloat16)
        return carry

    lax.fori_loop(0, 64, one, 0)
    surface[...] = jnp.zeros((4, PTS), jnp.float32)


def upward_part(pos, charge, count, up, outer, masked, turned, wide_points, wide_dens, order_ref):
    row = count[...].astype(jnp.float32)
    counted = column(row)
    masked[...] = jnp.where(
        iota((LEAF, PTS), 1).astype(jnp.float32) < counted, charge[...], 0.0
    )
    spots = [jnp.broadcast_to(column(outer[c : c + 1, :]), (TERMS, PTS)) for c in range(3)]
    lanes = iota((TERMS, PTS), 1)

    def leaf(n, check):
        source = masked[pl.ds(n, 1), :]
        square = jnp.full((TERMS, PTS), SOFTEN, jnp.float32)
        for c in range(3):
            spread = spots[c] - pos[c, pl.ds(n, 1), :]
            square = square + spread * spread
        total = jnp.sum(lax.rsqrt(square) * source, axis=1, keepdims=True)
        return jnp.where(lanes == n, total, check)

    check = lax.fori_loop(0, LEAF, leaf, jnp.zeros((TERMS, PTS), jnp.float32), unroll=16)
    dens = jnp.dot(up[...], check, preferred_element_type=jnp.float32, precision=EXACT_DOTS)
    turned[...] = jnp.transpose(jnp.concatenate([dens, dens], axis=0))
    even = turned[pl.ds(0, LEAF // 2, stride=2), :]
    odd = turned[pl.ds(1, LEAF // 2, stride=2), :]
    both = jnp.where(iota((LEAF // 2, PTS), 1) < TERMS, even, odd)
    for m in range(LEAF // 2):
        x, y, z = m // (CY * CZ // 2), m // (CZ // 2) % CY, m % (CZ // 2)
        wide_dens[x + 2, y + 2, z + 1] = both[m : m + 1]
    return row, counted


def points_part(pos, masked, wide_points):
    def line(x, y, carry):
        for z in range(CZ):
            n = (x * CY + y) * CZ + z
            rows = [pos[c, pl.ds(n, 1), :] for c in range(3)] + [masked[pl.ds(n, 1), :]]
            wide_points[x + 1, y + 1, z + 1] = jnp.concatenate(rows, axis=0)
        return carry

    over_plane(CX, CY, line, 0, CY)


def order_part(row, counted, order_ref):
    leaf = iota((LEAF, LEAF), 0).astype(jnp.float32)
    other = iota((LEAF, LEAF), 1).astype(jnp.float32)
    mine = counted * LEAF + leaf
    theirs = row * LEAF + other
    rank = jnp.sum(jnp.where(theirs < mine, 1.0, 0.0), axis=1, keepdims=True)
    order = jnp.sum(jnp.where(rank == other, leaf, 0.0), axis=0, keepdims=True)
    order_ref[...] = jnp.concatenate([order, order], axis=1).astype(jnp.int32)


def weights_part(inner, weights):
    upper_lanes = iota((TERMS, 2 * TERMS), 1) >= TERMS
    spread = []
    for c in range(3):
        row = inner[c : c + 1, :]
        spread.append(jnp.concatenate([row, row], axis=1) - column(row))
    squares_z = []
    for pair in range(PAIRS):
        shift = jnp.where(upper_lanes, float(pair + 1), float(pair - 3))
        squares_z.append((spread[2] - shift) * (spread[2] - shift))

    def line(n_x, n_y, carry):
        shift_x = n_x - 3
        shift_y = n_y - 3
        d_x = spread[0] - shift_x.astype(jnp.float32)
        d_y = spread[1] - shift_y.astype(jnp.float32)
        plane = d_x * d_x + d_y * d_y + SOFTEN
        close = jnp.maximum(jnp.abs(shift_x), jnp.abs(shift_y)) < 2
        for pair in range(PAIRS):
            weight = lax.rsqrt(plane + squares_z[pair])
            if pair == 0:
                weight = jnp.where(close & upper_lanes, 0.0, weight)
            if pair >= 2:
                weight = jnp.where(close & ~upper_lanes, 0.0, weight)
            high = weight.astype(jnp.bfloat16)
            at = ((n_x * 7 + n_y) * PAIRS + pair) * 2
            weights[at] = high
            weights[at + 1] = (weight - high.astype(jnp.float32)).astype(jnp.bfloat16)
        return carry

    over_plane(7, 7, line, 0, 7)


def gather_part(wide_dens, raw, grouped):
    half = iota((8, 2 * TERMS), 1) < TERMS
    blank = jnp.zeros((8, 2 * TERMS), jnp.float32)

    def gather(a_x, a_y, carry):
        for b in range(3):
            for parent in range(8):
                cell_x = 2 * (parent // 4) + a_x
                cell_y = 2 * (parent // 2 % 2) + a_y
                raw[a_x * 18 + a_y * 3 + b, parent : parent + 1, :] = wide_dens[
                    cell_x, cell_y, parent % 2 + b
                ]
        return carry

    over_plane(6, 6, gather, 0, 6)

    def split(a_x, a_y, carry):
        layers = [blank]
        for b in range(3):
            value = raw[a_x * 18 + a_y * 3 + b]
            swapped = pltpu.roll(value, TERMS, 1)
            for twice in (jnp.where(half, value, swapped), jnp.where(half, swapped, value)):
                high = rounded(twice)
                layers.append(jnp.where(half, high, twice - high))
        layers.append(blank)
        for at in range(7):
            grouped[(a_x + 1) * 8 + a_y + 1, at] = jnp.concatenate(
                layers[at : at + 2], axis=0
            ).astype(jnp.bfloat16)
        return carry

    over_plane(6, 6, split, 0, 6)


def translate_part(weights, grouped, down_ref, local):
    def plane(n_x, total):
        lefts = []
        rights = []
        for n_y in range(7):
            for pair in range(PAIRS):
                pieces = []
                for at in (pair, pair + 4):
                    for parity in range(4):
                        pieces.append(grouped[(n_x + parity // 2) * 8 + n_y + parity % 2, at])
                lefts.append(jnp.concatenate(pieces, axis=0))
                at = ((n_x * 7 + n_y) * PAIRS + pair) * 2
                right = jnp.concatenate([weights[at], weights[at + 1]], axis=1)
                rights += [right, right]
        return total + jnp.dot(
            jnp.concatenate(lefts, axis=1),
            jnp.concatenate(rights, axis=0),
            preferred_element_type=jnp.float32,
        )

    total = lax.fori_loop(0, 7, plane, jnp.zeros((2 * LEAF, 4 * TERMS), jnp.float32))
    total = total[:, : 2 * TERMS] + total[:, 2 * TERMS :]
    total = jnp.where(iota((LEAF, 2 * TERMS), 1) < TERMS, total[:LEAF], total[LEAF:])
    down = down_ref[...]
    down = jnp.concatenate([down, down], axis=1)
    down = jnp.concatenate([down, jnp.zeros_like(down)], axis=0)
    local[...] = lax.dot_general(
        total,
        down,
        (((1,), (1,)), ((), ())),
        preferred_element_type=jnp.float32,
        precision=EXACT_DOTS,
    )


def gather_body(
    pos_hbm,
    charge_hbm,
    count_hbm,
    up_hbm,
    down_hbm,
    inner_hbm,
    outer_hbm,
    wide_points,
    sources,
    targets,
    local,
    order_ref,
    wide_dens,
    pos,
    charge,
    count,
    up,
    down,
    inner,
    outer,
    masked,
    turned,
    weights,
    raw,
    grouped,
    surface,
    load_sem,
    send_sem,
    recv_sem,
):
    low_bits, mid_bits, high_bits = axis_bits()
    total_bits = low_bits + mid_bits + high_bits
    device = (
        lax.axis_index("gx") * 2**mid_bits + lax.axis_index("gy")
    ) * 2**low_bits + lax.axis_index("gz")
    place = []
    extent = []
    for c in range(3):
        bits = list(range(c, total_bits, 3))
        place.append(sum((device // 2**bit % 2) * 2**rank for rank, bit in enumerate(bits)))
        extent.append(2 ** len(bits))

    def there(side):
        inside = jnp.bool_(True)
        for c in range(3):
            if side[c] > 0:
                inside = inside & (place[c] < extent[c] - 1)
            if side[c] < 0:
                inside = inside & (place[c] > 0)
        return inside

    def coordinates(side):
        other = 0
        for c in range(3):
            moved = place[c] + side[c]
            for rank, bit in enumerate(range(c, total_bits, 3)):
                other = other + (moved // 2**rank % 2) * 2**bit
        return (
            other // 2 ** (low_bits + mid_bits),
            other // 2**low_bits % 2**mid_bits,
            other % 2**low_bits,
        )

    kinds = (
        (wide_dens, (CX, CY, CZ // 2), (2, 2, 1)),
        (wide_points, (CX, CY, CZ), (1, 1, 1)),
    )

    def regions(kind, at):
        wide, sizes, layers = kinds[kind]
        return zip(*(rim(SIDES[at][c], sizes[c], layers[c]) for c in range(3)))

    def remote(kind, at):
        wide = kinds[kind][0]
        source, target = regions(kind, at)
        return pltpu.make_async_remote_copy(
            src_ref=wide.at[source],
            dst_ref=wide.at[target],
            send_sem=send_sem.at[kind, at],
            recv_sem=recv_sem.at[kind, at],
            device_id=coordinates(SIDES[at]),
            device_id_type=pl.DeviceIdType.MESH,
        )

    loads = [
        pltpu.make_async_copy(source, target, load_sem.at[at])
        for at, (source, target) in enumerate(
            (
                (pos_hbm, pos),
                (charge_hbm, charge),
                (count_hbm, count),
                (outer_hbm, outer),
                (up_hbm, up),
                (inner_hbm, inner),
                (down_hbm, down),
            )
        )
    ]
    for load in loads:
        load.start()
    barrier = pltpu.get_barrier_semaphore()
    met = jnp.int32(0)
    order = sorted(range(len(SIDES)), key=lambda at: -sum(map(abs, SIDES[at])))
    for at in order:
        inside = there(SIDES[at])
        met = met + jnp.where(inside, 1, 0)

        @pl.when(inside)
        def _(at=at):
            pl.semaphore_signal(
                barrier,
                inc=1,
                device_id=coordinates(SIDES[at]),
                device_id_type=pl.DeviceIdType.MESH,
            )

    clear_part(grouped, surface)
    for load in loads:
        load.wait()
    surface[0:3, 0:TERMS] = outer[...]
    row, counted = upward_part(
        pos, charge, count, up, outer, masked, turned, wide_points, wide_dens, order_ref
    )
    pl.semaphore_wait(barrier, met)

    def send(kind):
        for at in order:

            @pl.when(there(SIDES[at]))
            def _(at=at):
                remote(kind, at).start()

    def finish(kind):
        for at in order:

            @pl.when(there(SIDES[at]))
            def _(at=at):
                remote(kind, at).wait_send()

            @pl.when(there(tuple(-c for c in SIDES[at])))
            def _(at=at):
                remote(kind, at).wait_recv()

    def blank(kind):
        for at in order:

            @pl.when(~there(tuple(-c for c in SIDES[at])))
            def _(at=at):
                wide = kinds[kind][0]
                _, target = regions(kind, at)
                shape = tuple(piece.size for piece in target) + wide.shape[3:]
                wide[target] = jnp.zeros(shape, jnp.float32)

    send(0)
    points_part(pos, masked, wide_points)
    send(1)
    order_part(row, counted, order_ref)
    blank(0)
    blank(1)
    weights_part(inner, weights)

    def source(e_x, e_y, e_z):
        n = (e_x * (CY + 2) + e_y) * (CZ + 2) + e_z
        sources[n] = source_features(
            wide_points[e_x, e_y, e_z], middle(e_x), middle(e_y), middle(e_z)
        )

    def prepare_own(x, y, carry):
        for z in range(CZ):
            n = (x * CY + y) * CZ + z
            spot = (middle(x + 1), middle(y + 1), middle(z + 1))
            points = wide_points[x + 1, y + 1, z + 1]
            targets[n] = target_features(points, *spot)
            sources[ext_index(x, y, z)] = source_features(points, *spot)
            sources[EXT + n] = source_features(surface[...], *spot)
        return carry

    over_plane(CX, CY, prepare_own, 0, CY)
    finish(0)
    gather_part(wide_dens, raw, grouped)
    translate_part(weights, grouped, down, local)
    finish(1)

    def prepare_ends(y, carry):
        for e_x in (0, CX + 1):
            for e_z in range(CZ + 2):
                source(e_x, y, e_z)
        return carry

    def prepare_sides(x, carry):
        for e_y in (0, CY + 1):
            for e_z in range(CZ + 2):
                source(x, e_y, e_z)
        for e_y in range(1, CY + 1):
            for e_z in (0, CZ + 1):
                source(x, e_y, e_z)
        return carry

    lax.fori_loop(0, CY + 2, prepare_ends, 0)
    lax.fori_loop(1, CX + 1, prepare_sides, 0)


def near_body(count_ref, order_ref, points_ref, sources, targets, local, out_ref):
    lane = iota((1, PTS), 1)

    def leaf(n):
        x, y, z = n >> 4, (n >> 2) & 3, n & 3
        base = ext_index(x, y, z)
        parity = (x & 1) * 4 + (y & 1) * 2 + (z & 1)
        parent = (x >> 1) * 4 + (y >> 1) * 2 + (z >> 1)
        count = count_ref[n]
        blocks = []
        for s_x in range(-1, 2):
            for s_y in range(-1, 2):
                for s_z in range(-1, 2):
                    blocks.append(base + s_x * ((CY + 2) * (CZ + 2)) + s_y * (CZ + 2) + s_z)

        def rows(size):
            left = targets[n, 0:size, :]
            eye = iota((size, PTS), 0) == iota((size, PTS), 1)
            total = jnp.zeros((size, PTS), jnp.float32)
            for at in range(0, 28, 2):
                right = []
                charge = []
                for b in (at, at + 1):
                    if b < 27:
                        right.append(sources[blocks[b]])
                        charge.append(points_ref[blocks[b], 3:4, :])
                    else:
                        right.append(sources[EXT + n])
                        charge.append(local[pl.ds(parity * 8 + parent, 1), :])
                square = jnp.dot(
                    left, jnp.concatenate(right, axis=1), preferred_element_type=jnp.float32
                )
                weight = lax.rsqrt(square)
                for k, b in enumerate((at, at + 1)):
                    part = weight[:, k * PTS : (k + 1) * PTS]
                    if b == 13:
                        part = jnp.where(eye, 0.0, part)
                    total = total + part * charge[k]
            sums = jnp.sum(total, axis=1, keepdims=True)
            flat = jnp.sum(jnp.where(eye, sums, 0.0), axis=0, keepdims=True)
            out_ref[pl.ds(n, 1), :] = jnp.where(lane < count, flat, 0.0)

        return (count + 15) >> 4, rows

    def leaf_group(g, carry):
        group = [leaf(order_ref[0, g * LINE + k]) for k in range(LINE)]
        most = group[0][0]
        for filled, _ in group[1:]:
            most = jnp.maximum(most, filled)

        def together(size):
            for _, rows in group:
                rows(size)

        for k in range(1, 9):
            pl.when(most == k)(partial(together, 16 * k))
        return carry

    lax.fori_loop(0, LEAF // LINE, leaf_group, 0)


def gather_all(positions, charges, counts, up_inverse, down_inverse, inner_surface, outer_surface):
    wide = (CX + 2, CY + 2, CZ + 2, 4, PTS)
    return pl.pallas_call(
        gather_body,
        out_shape=(
            pltpu.VMEM(wide, jnp.float32),
            pltpu.VMEM((EXT + LEAF, FEATS, PTS), jnp.bfloat16),
            pltpu.VMEM((LEAF, PTS, FEATS), jnp.bfloat16),
            pltpu.VMEM((LEAF, 2 * TERMS), jnp.float32),
            pltpu.VMEM((1, 2 * LEAF), jnp.int32),
        ),
        in_specs=[anywhere()] * 7,
        out_specs=(whole(),) * 5,
        scratch_shapes=[
            pltpu.VMEM((CX + 4, CY + 4, CZ // 2 + 2, 1, 2 * TERMS), jnp.float32),
            pltpu.VMEM((3, LEAF, PTS), jnp.float32),
            pltpu.VMEM((LEAF, PTS), jnp.float32),
            pltpu.VMEM((1, LEAF), jnp.int32),
            pltpu.VMEM((TERMS, TERMS), jnp.float32),
            pltpu.VMEM((TERMS, TERMS), jnp.float32),
            pltpu.VMEM((3, TERMS), jnp.float32),
            pltpu.VMEM((3, TERMS), jnp.float32),
            pltpu.VMEM((LEAF, PTS), jnp.float32),
            pltpu.VMEM((PTS, 2 * TERMS), jnp.float32),
            pltpu.VMEM((49 * PAIRS * 2, TERMS, 2 * TERMS), jnp.bfloat16),
            pltpu.VMEM((108, 8, 2 * TERMS), jnp.float32),
            pltpu.VMEM((64, 8, 16, 2 * TERMS), jnp.bfloat16),
            pltpu.VMEM((4, PTS), jnp.float32),
            pltpu.SemaphoreType.DMA((7,)),
            pltpu.SemaphoreType.DMA((2, len(SIDES))),
            pltpu.SemaphoreType.DMA((2, len(SIDES))),
        ],
        compiler_params=pltpu.CompilerParams(
            collective_id=0, has_side_effects=True, vmem_limit_bytes=32 * 2**20
        ),
        name="gather",
    )(positions, charges, counts, up_inverse, down_inverse, inner_surface, outer_surface)


def potentials(counts, order, points, sources, targets, local):
    return pl.pallas_call(
        near_body,
        out_shape=jax.ShapeDtypeStruct((LEAF, PTS), jnp.float32),
        in_specs=[scalars()] * 2 + [whole()] * 4,
        out_specs=whole(),
        compiler_params=pltpu.CompilerParams(vmem_limit_bytes=32 * 2**20),
        name="potentials",
    )(counts, order, points, sources, targets, local)


def per_device(positions, charges, counts, up_inverse, down_inverse, inner_surface, outer_surface):
    points, sources, targets, local, order = gather_all(
        jnp.transpose(positions, (1, 0, 2)),
        charges,
        counts.reshape(1, LEAF),
        up_inverse,
        down_inverse,
        inner_surface,
        outer_surface,
    )
    return potentials(counts, order, points.reshape(EXT, 4, PTS), sources, targets, local)


def solution(mesh):
    in_specs = (
        P(("gx", "gy", "gz"), None, None),
        P(("gx", "gy", "gz"), None),
        P(("gx", "gy", "gz")),
        P(),
        P(),
        P(),
        P(),
    )
    out_specs = P(("gx", "gy", "gz"), None)
    return jax.shard_map(
        per_device, mesh=mesh, in_specs=in_specs, out_specs=out_specs, check_vma=False
    )
```

```python
from functools import partial

import jax
import jax.numpy as jnp
from jax import lax
from jax.experimental import pallas as pl
from jax.experimental.pallas import tpu as pltpu
from jax.sharding import PartitionSpec as P

CX = 4
CY = 4
CZ = 4
PTS = 128
TERMS = 64
LEAF = CX * CY * CZ
EXT = (CX + 2) * (CY + 2) * (CZ + 2)
FEATS = 32
LINE = 4
PAIRS = 4


SOFTEN = 0.0025
EXACT_DOTS = lax.Precision.HIGHEST


def iota(shape, dimension):
    return lax.broadcasted_iota(jnp.int32, shape, dimension)


def column(row):
    size = row.shape[1]
    eye = iota((size, size), 0) == iota((size, size), 1)
    return jnp.sum(jnp.where(eye, row, 0.0), axis=1, keepdims=True)


def over_plane(size_x, size_y, body, start, unroll=1):
    def line(x, carry):
        return lax.fori_loop(0, size_y, lambda y, held: body(x, y, held), carry, unroll=unroll)

    return lax.fori_loop(0, size_x, line, start)


def rounded(value):
    return value.astype(jnp.bfloat16).astype(jnp.float32)


def three_parts(value):
    high = rounded(value)
    middle = rounded(value - high)
    low = rounded(value - high - middle)
    return high, middle, low


def squares_of(points, shift_x, shift_y, shift_z, extra):
    row = iota((8, PTS), 0) % 4
    twice = jnp.concatenate([points, points], axis=0)
    place = twice + jnp.where(row == 0, shift_x, jnp.where(row == 1, shift_y, shift_z))
    square = place * place
    norm = square[0:1] + square[1:2] + square[2:3] + extra
    return jnp.where(row == 3, norm, place), row == 3, iota((8, PTS), 0) < 4


def source_features(points, shift_x, shift_y, shift_z):
    value, last, first = squares_of(points, shift_x, shift_y, shift_z, 0.0)
    high, middle, low = three_parts(value)
    scale = jnp.where(last, 1.0, -2.0)
    high_one = jnp.where(last, 1.0, -2.0 * high)
    middle_one = jnp.where(last, 1.0, -2.0 * middle)
    rows = [
        jnp.where(first, high * scale, middle * scale),
        jnp.where(first, low * scale, high_one),
        jnp.where(first, high_one, middle_one),
        jnp.zeros((8, PTS), jnp.float32),
    ]
    return jnp.concatenate(rows, axis=0).astype(jnp.bfloat16)


def target_features(points, shift_x, shift_y, shift_z):
    value, last, first = squares_of(points, shift_x, shift_y, shift_z, SOFTEN)
    high, middle, low = three_parts(value)
    high_one = jnp.where(last, 1.0, high)
    rows = [
        high_one,
        jnp.where(first, high_one, jnp.where(last, high, middle)),
        jnp.where(first, jnp.where(last, middle, low), jnp.where(last, low, middle)),
        jnp.zeros((8, PTS), jnp.float32),
    ]
    return jnp.transpose(jnp.concatenate(rows, axis=0)).astype(jnp.bfloat16)


def whole():
    return pl.BlockSpec(memory_space=pltpu.VMEM)


def scalars():
    return pl.BlockSpec(memory_space=pltpu.SMEM)


def anywhere():
    return pl.BlockSpec(memory_space=pl.ANY)


def axis_bits():
    low_bits = lax.axis_size("gz").bit_length() - 1
    mid_bits = lax.axis_size("gy").bit_length() - 1
    high_bits = lax.axis_size("gx").bit_length() - 1
    return (low_bits, mid_bits, high_bits)


SIDES = [
    (x, y, z)
    for x in (-1, 0, 1)
    for y in (-1, 0, 1)
    for z in (-1, 0, 1)
    if (x, y, z) != (0, 0, 0)
]


def rim(side, size, layers):
    if side > 0:
        return pl.ds(size, layers), pl.ds(0, layers)
    if side < 0:
        return pl.ds(layers, layers), pl.ds(size + layers, layers)
    return pl.ds(layers, size), pl.ds(layers, size)


def middle(cell):
    if isinstance(cell, int):
        return jnp.float32(cell) - (CX // 2 + 1)
    return cell.astype(jnp.float32) - (CX // 2 + 1)


def ext_index(x, y, z):
    return ((x + 1) * (CY + 2) + y + 1) * (CZ + 2) + z + 1


def clear_part(grouped, surface):
    def one(n, carry):
        grouped[n] = jnp.zeros((8, 16, 2 * TERMS), jnp.bfloat16)
        return carry

    lax.fori_loop(0, 64, one, 0)
    surface[...] = jnp.zeros((4, PTS), jnp.float32)


def upward_part(pos, charge, count, up, outer, masked, turned, wide_points, wide_dens, order_ref):
    row = count[...].astype(jnp.float32)
    counted = column(row)
    masked[...] = jnp.where(
        iota((LEAF, PTS), 1).astype(jnp.float32) < counted, charge[...], 0.0
    )
    spots = [jnp.broadcast_to(column(outer[c : c + 1, :]), (TERMS, PTS)) for c in range(3)]
    lanes = iota((TERMS, PTS), 1)

    def leaf(n, check):
        source = masked[pl.ds(n, 1), :]
        square = jnp.full((TERMS, PTS), SOFTEN, jnp.float32)
        for c in range(3):
            spread = spots[c] - pos[c, pl.ds(n, 1), :]
            square = square + spread * spread
        total = jnp.sum(lax.rsqrt(square) * source, axis=1, keepdims=True)
        return jnp.where(lanes == n, total, check)

    check = lax.fori_loop(0, LEAF, leaf, jnp.zeros((TERMS, PTS), jnp.float32), unroll=16)
    dens = jnp.dot(up[...], check, preferred_element_type=jnp.float32, precision=EXACT_DOTS)
    turned[...] = jnp.transpose(jnp.concatenate([dens, dens], axis=0))
    even = turned[pl.ds(0, LEAF // 2, stride=2), :]
    odd = turned[pl.ds(1, LEAF // 2, stride=2), :]
    both = jnp.where(iota((LEAF // 2, PTS), 1) < TERMS, even, odd)
    for m in range(LEAF // 2):
        x, y, z = m // (CY * CZ // 2), m // (CZ // 2) % CY, m % (CZ // 2)
        wide_dens[x + 2, y + 2, z + 1] = both[m : m + 1]
    return row, counted


def points_part(pos, masked, wide_points):
    def line(x, y, carry):
        for z in range(CZ):
            n = (x * CY + y) * CZ + z
            rows = [pos[c, pl.ds(n, 1), :] for c in range(3)] + [masked[pl.ds(n, 1), :]]
            wide_points[x + 1, y + 1, z + 1] = jnp.concatenate(rows, axis=0)
        return carry

    over_plane(CX, CY, line, 0, CY)


def order_part(row, counted, order_ref):
    leaf = iota((LEAF, LEAF), 0).astype(jnp.float32)
    other = iota((LEAF, LEAF), 1).astype(jnp.float32)
    mine = counted * LEAF + leaf
    theirs = row * LEAF + other
    rank = jnp.sum(jnp.where(theirs < mine, 1.0, 0.0), axis=1, keepdims=True)
    order = jnp.sum(jnp.where(rank == other, leaf, 0.0), axis=0, keepdims=True)
    order_ref[...] = jnp.concatenate([order, row], axis=1).astype(jnp.int32)


def weights_part(inner, weights):
    upper_lanes = iota((TERMS, 2 * TERMS), 1) >= TERMS
    spread = []
    for c in range(3):
        row = inner[c : c + 1, :]
        spread.append(jnp.concatenate([row, row], axis=1) - column(row))
    squares_z = []
    for pair in range(PAIRS):
        shift = jnp.where(upper_lanes, float(pair + 1), float(pair - 3))
        squares_z.append((spread[2] - shift) * (spread[2] - shift))

    def line(n_x, n_y, carry):
        shift_x = n_x - 3
        shift_y = n_y - 3
        d_x = spread[0] - shift_x.astype(jnp.float32)
        d_y = spread[1] - shift_y.astype(jnp.float32)
        plane = d_x * d_x + d_y * d_y + SOFTEN
        close = jnp.maximum(jnp.abs(shift_x), jnp.abs(shift_y)) < 2
        for pair in range(PAIRS):
            weight = lax.rsqrt(plane + squares_z[pair])
            if pair == 0:
                weight = jnp.where(close & upper_lanes, 0.0, weight)
            if pair >= 2:
                weight = jnp.where(close & ~upper_lanes, 0.0, weight)
            high = weight.astype(jnp.bfloat16)
            low = (weight - high.astype(jnp.float32)).astype(jnp.bfloat16)
            at = (n_x * 7 + n_y) * 2
            weights[at, pair * TERMS : (pair + 1) * TERMS] = high
            weights[at + 1, pair * TERMS : (pair + 1) * TERMS] = low
        return carry

    over_plane(7, 7, line, 0, 7)


def gather_part(wide_dens, raw, grouped):
    half = iota((8, 2 * TERMS), 1) < TERMS
    blank = jnp.zeros((8, 2 * TERMS), jnp.float32)

    def gather(a_x, a_y, carry):
        for b in range(3):
            for parent in range(8):
                cell_x = 2 * (parent // 4) + a_x
                cell_y = 2 * (parent // 2 % 2) + a_y
                raw[a_x * 18 + a_y * 3 + b, parent : parent + 1, :] = wide_dens[
                    cell_x, cell_y, parent % 2 + b
                ]
        return carry

    over_plane(6, 6, gather, 0, 6)

    def split(a_x, a_y, carry):
        whole_rows = []
        for b in range(3):
            value = raw[a_x * 18 + a_y * 3 + b]
            high = rounded(value)
            whole_rows.append((high, value - high))
        for part in range(2):
            first, second, third = (member[part] for member in whole_rows)
            one, two, three = (pltpu.roll(member, TERMS, 1) for member in (first, second, third))
            tiles = [
                (jnp.where(half, 0.0, one), first),
                (jnp.where(half, one, two), second),
                (jnp.where(half, two, three), third),
                (jnp.where(half, three, 0.0), blank),
            ]
            for at, rows in enumerate(tiles):
                grouped[(a_x + 1) * 8 + a_y + 1, 4 * part + at] = jnp.concatenate(
                    rows, axis=0
                ).astype(jnp.bfloat16)
        return carry

    over_plane(6, 6, split, 0, 6)


def translate_part(weights, grouped, down_ref, local):
    def product(places, parities):
        lefts = []
        rights = []
        for n_x, n_y in places:
            for lanes in range(2):
                pieces = []
                for kind in (0, 4, 2, 6):
                    for parity in parities:
                        at = (n_x + parity // 2) * 8 + n_y + parity % 2
                        pieces.append(grouped[at, kind + lanes])
                lefts.append(jnp.concatenate(pieces, axis=0))
            at = (n_x * 7 + n_y) * 2
            rights.append(jnp.concatenate([weights[at], weights[at + 1]], axis=1))
        result = jnp.dot(
            jnp.concatenate(lefts, axis=1),
            jnp.concatenate(rights, axis=0),
            preferred_element_type=jnp.float32,
        )
        for kind in range(4):
            for k, parity in enumerate(parities):
                at = (kind * len(parities) + k) * 16
                sums[kind * 4 + parity].append(result[at : at + 16])

    sums = [[] for _ in range(16)]
    inner_shifts = range(1, 6)
    product([(n_x, n_y) for n_x in inner_shifts for n_y in inner_shifts], (0, 1, 2, 3))
    product([(0, n_y) for n_y in range(7)], (2, 3))
    product([(6, n_y) for n_y in range(7)], (0, 1))
    product([(n_x, 0) for n_x in inner_shifts], (1, 3))
    product([(n_x, 6) for n_x in inner_shifts], (0, 2))
    total = jnp.concatenate([sum(rows[1:], rows[0]) for rows in sums], axis=0)
    total = total[:, : 2 * TERMS] + total[:, 2 * TERMS :]
    lower = total[:LEAF] + total[LEAF : 2 * LEAF]
    upper = total[2 * LEAF : 3 * LEAF] + total[3 * LEAF :]
    total = jnp.where(iota((LEAF, 2 * TERMS), 1) < TERMS, lower, upper)
    down = down_ref[...]
    down = jnp.concatenate([down, down], axis=1)
    down = jnp.concatenate([down, jnp.zeros_like(down)], axis=0)
    local[...] = lax.dot_general(
        total,
        down,
        (((1,), (1,)), ((), ())),
        preferred_element_type=jnp.float32,
        precision=EXACT_DOTS,
    )


def gather_body(
    pos_hbm,
    charge_hbm,
    count_hbm,
    up_hbm,
    down_hbm,
    inner_hbm,
    outer_hbm,
    wide_points,
    sources,
    targets,
    local,
    order_ref,
    wide_dens,
    pos,
    charge,
    count,
    up,
    down,
    inner,
    outer,
    masked,
    turned,
    weights,
    raw,
    grouped,
    surface,
    load_sem,
    send_sem,
    recv_sem,
):
    low_bits, mid_bits, high_bits = axis_bits()
    total_bits = low_bits + mid_bits + high_bits
    device = (
        lax.axis_index("gx") * 2**mid_bits + lax.axis_index("gy")
    ) * 2**low_bits + lax.axis_index("gz")
    place = []
    extent = []
    for c in range(3):
        bits = list(range(c, total_bits, 3))
        place.append(sum((device // 2**bit % 2) * 2**rank for rank, bit in enumerate(bits)))
        extent.append(2 ** len(bits))

    steps = []
    for c in range(3):
        moves = {}
        for move in (-1, 0, 1):
            moved = place[c] + move
            spot = [0, 0, 0]
            for rank, bit in enumerate(range(c, total_bits, 3)):
                digit = moved // 2**rank % 2
                if bit < low_bits:
                    spot[2] = spot[2] + digit * 2**bit
                elif bit < low_bits + mid_bits:
                    spot[1] = spot[1] + digit * 2 ** (bit - low_bits)
                else:
                    spot[0] = spot[0] + digit * 2 ** (bit - low_bits - mid_bits)
            moves[move] = spot
        steps.append(moves)
    room = [{1: place[c] < extent[c] - 1, -1: place[c] > 0} for c in range(3)]
    inside = {}
    for side in SIDES:
        held = None
        for c in range(3):
            if side[c] != 0:
                held = room[c][side[c]] if held is None else held & room[c][side[c]]
        inside[side] = held

    def there(side):
        return inside[side]

    def coordinates(side):
        return tuple(
            sum(steps[c][side[c]][axis] for c in range(3)) + jnp.int32(0) for axis in range(3)
        )

    kinds = (
        (wide_dens, (CX, CY, CZ // 2), (2, 2, 1)),
        (wide_points, (CX, CY, CZ), (1, 1, 1)),
    )

    def regions(kind, at):
        wide, sizes, layers = kinds[kind]
        return zip(*(rim(SIDES[at][c], sizes[c], layers[c]) for c in range(3)))

    def remote(kind, at):
        wide = kinds[kind][0]
        source, target = regions(kind, at)
        return pltpu.make_async_remote_copy(
            src_ref=wide.at[source],
            dst_ref=wide.at[target],
            send_sem=send_sem.at[kind, at],
            recv_sem=recv_sem.at[kind, at],
            device_id=coordinates(SIDES[at]),
            device_id_type=pl.DeviceIdType.MESH,
        )

    loads = [
        pltpu.make_async_copy(source, target, load_sem.at[at])
        for at, (source, target) in enumerate(
            (
                (pos_hbm, pos),
                (charge_hbm, charge),
                (count_hbm, count),
                (outer_hbm, outer),
                (up_hbm, up),
                (inner_hbm, inner),
                (down_hbm, down),
            )
        )
    ]
    for load in loads:
        load.start()
    barrier = pltpu.get_barrier_semaphore()
    met = jnp.int32(0)
    order = sorted(range(len(SIDES)), key=lambda at: -sum(map(abs, SIDES[at])))
    for at in order:
        met = met + jnp.where(there(SIDES[at]), 1, 0)

        @pl.when(there(SIDES[at]))
        def _(at=at):
            pl.semaphore_signal(
                barrier,
                inc=1,
                device_id=coordinates(SIDES[at]),
                device_id_type=pl.DeviceIdType.MESH,
            )

    clear_part(grouped, surface)
    for load in loads:
        load.wait()
    surface[0:3, 0:TERMS] = outer[...]
    row, counted = upward_part(
        pos, charge, count, up, outer, masked, turned, wide_points, wide_dens, order_ref
    )
    pl.semaphore_wait(barrier, met)

    def send(kind):
        for at in order:

            @pl.when(there(SIDES[at]))
            def _(at=at):
                remote(kind, at).start()

    def finish(kind):
        for at in order:

            @pl.when(there(SIDES[at]))
            def _(at=at):
                remote(kind, at).wait_send()

            @pl.when(there(tuple(-c for c in SIDES[at])))
            def _(at=at):
                remote(kind, at).wait_recv()

    def blank(kind):
        for at in order:

            @pl.when(~there(tuple(-c for c in SIDES[at])))
            def _(at=at):
                wide = kinds[kind][0]
                _, target = regions(kind, at)
                shape = tuple(piece.size for piece in target) + wide.shape[3:]
                wide[target] = jnp.zeros(shape, jnp.float32)

    send(0)
    points_part(pos, masked, wide_points)
    send(1)
    order_part(row, counted, order_ref)
    blank(0)
    blank(1)
    weights_part(inner, weights)

    def source(e_x, e_y, e_z):
        n = (e_x * (CY + 2) + e_y) * (CZ + 2) + e_z
        sources[n] = source_features(
            wide_points[e_x, e_y, e_z], middle(e_x), middle(e_y), middle(e_z)
        )

    def prepare_own(x, y, carry):
        for z in range(CZ):
            n = (x * CY + y) * CZ + z
            spot = (middle(x + 1), middle(y + 1), middle(z + 1))
            points = wide_points[x + 1, y + 1, z + 1]
            targets[n] = target_features(points, *spot)
            sources[ext_index(x, y, z)] = source_features(points, *spot)
            sources[EXT + n] = source_features(surface[...], *spot)
        return carry

    over_plane(CX, CY, prepare_own, 0, CY)
    finish(0)
    gather_part(wide_dens, raw, grouped)
    translate_part(weights, grouped, down, local)
    finish(1)

    def prepare_ends(y, carry):
        for e_x in (0, CX + 1):
            for e_z in range(CZ + 2):
                source(e_x, y, e_z)
        return carry

    def prepare_sides(x, carry):
        for e_y in (0, CY + 1):
            for e_z in range(CZ + 2):
                source(x, e_y, e_z)
        for e_y in range(1, CY + 1):
            for e_z in (0, CZ + 1):
                source(x, e_y, e_z)
        return carry

    lax.fori_loop(0, CY + 2, prepare_ends, 0)
    lax.fori_loop(1, CX + 1, prepare_sides, 0)


def near_body(order_ref, points_ref, sources, targets, local, out_ref):
    lane = iota((1, PTS), 1)

    def leaf(n):
        x, y, z = n >> 4, (n >> 2) & 3, n & 3
        base = ext_index(x, y, z)
        parity = (x & 1) * 4 + (y & 1) * 2 + (z & 1)
        parent = (x >> 1) * 4 + (y >> 1) * 2 + (z >> 1)
        count = order_ref[0, LEAF + n]
        blocks = []
        for s_x in range(-1, 2):
            for s_y in range(-1, 2):
                for s_z in range(-1, 2):
                    blocks.append(base + s_x * ((CY + 2) * (CZ + 2)) + s_y * (CZ + 2) + s_z)

        def rows(size):
            left = targets[n, 0:size, :]
            eye = iota((size, PTS), 0) == iota((size, PTS), 1)
            total = jnp.zeros((size, PTS), jnp.float32)
            for at in range(0, 28, 2):
                right = []
                charge = []
                for b in (at, at + 1):
                    if b < 27:
                        right.append(sources[blocks[b]])
                        charge.append(points_ref[blocks[b], 3:4, :])
                    else:
                        right.append(sources[EXT + n])
                        charge.append(local[pl.ds(parity * 8 + parent, 1), :])
                square = jnp.dot(
                    left, jnp.concatenate(right, axis=1), preferred_element_type=jnp.float32
                )
                weight = lax.rsqrt(square)
                for k, b in enumerate((at, at + 1)):
                    part = weight[:, k * PTS : (k + 1) * PTS]
                    if b == 13:
                        part = jnp.where(eye, 0.0, part)
                    total = total + part * charge[k]
            sums = jnp.sum(total, axis=1, keepdims=True)
            flat = jnp.sum(jnp.where(eye, sums, 0.0), axis=0, keepdims=True)
            out_ref[pl.ds(n, 1), :] = jnp.where(lane < count, flat, 0.0)

        return (count + 15) >> 4, rows

    def leaf_group(g, carry):
        group = [leaf(order_ref[0, g * LINE + k]) for k in range(LINE)]
        most = group[0][0]
        for filled, _ in group[1:]:
            most = jnp.maximum(most, filled)

        def together(size):
            for _, rows in group:
                rows(size)

        for k in range(1, 9):
            pl.when(most == k)(partial(together, 16 * k))
        return carry

    lax.fori_loop(0, LEAF // LINE, leaf_group, 0)


def gather_all(positions, charges, counts, up_inverse, down_inverse, inner_surface, outer_surface):
    wide = (CX + 2, CY + 2, CZ + 2, 4, PTS)
    return pl.pallas_call(
        gather_body,
        out_shape=(
            pltpu.VMEM(wide, jnp.float32),
            pltpu.VMEM((EXT + LEAF, FEATS, PTS), jnp.bfloat16),
            pltpu.VMEM((LEAF, PTS, FEATS), jnp.bfloat16),
            pltpu.VMEM((LEAF, 2 * TERMS), jnp.float32),
            pltpu.VMEM((1, 2 * LEAF), jnp.int32),
        ),
        in_specs=[anywhere()] * 7,
        out_specs=(whole(),) * 5,
        scratch_shapes=[
            pltpu.VMEM((CX + 4, CY + 4, CZ // 2 + 2, 1, 2 * TERMS), jnp.float32),
            pltpu.VMEM((3, LEAF, PTS), jnp.float32),
            pltpu.VMEM((LEAF, PTS), jnp.float32),
            pltpu.VMEM((1, LEAF), jnp.int32),
            pltpu.VMEM((TERMS, TERMS), jnp.float32),
            pltpu.VMEM((TERMS, TERMS), jnp.float32),
            pltpu.VMEM((3, TERMS), jnp.float32),
            pltpu.VMEM((3, TERMS), jnp.float32),
            pltpu.VMEM((LEAF, PTS), jnp.float32),
            pltpu.VMEM((PTS, 2 * TERMS), jnp.float32),
            pltpu.VMEM((98, PAIRS * TERMS, 2 * TERMS), jnp.bfloat16),
            pltpu.VMEM((108, 8, 2 * TERMS), jnp.float32),
            pltpu.VMEM((64, 8, 16, 2 * TERMS), jnp.bfloat16),
            pltpu.VMEM((4, PTS), jnp.float32),
            pltpu.SemaphoreType.DMA((7,)),
            pltpu.SemaphoreType.DMA((2, len(SIDES))),
            pltpu.SemaphoreType.DMA((2, len(SIDES))),
        ],
        compiler_params=pltpu.CompilerParams(
            collective_id=0, has_side_effects=True, vmem_limit_bytes=32 * 2**20
        ),
        name="gather",
    )(positions, charges, counts, up_inverse, down_inverse, inner_surface, outer_surface)


def potentials(order, points, sources, targets, local):
    return pl.pallas_call(
        near_body,
        out_shape=jax.ShapeDtypeStruct((LEAF, PTS), jnp.float32),
        in_specs=[scalars()] + [whole()] * 4,
        out_specs=whole(),
        compiler_params=pltpu.CompilerParams(vmem_limit_bytes=32 * 2**20),
        name="potentials",
    )(order, points, sources, targets, local)


def per_device(positions, charges, counts, up_inverse, down_inverse, inner_surface, outer_surface):
    arguments = (
        jnp.transpose(positions, (1, 0, 2)),
        charges,
        counts.reshape(1, LEAF),
        up_inverse,
        down_inverse,
        inner_surface,
        outer_surface,
    )
    points, sources, targets, local, order = gather_all(
        *(pltpu.with_memory_space_constraint(member, pltpu.HBM) for member in arguments)
    )
    return potentials(order, points.reshape(EXT, 4, PTS), sources, targets, local)


def solution(mesh):
    in_specs = (
        P(("gx", "gy", "gz"), None, None),
        P(("gx", "gy", "gz"), None),
        P(("gx", "gy", "gz")),
        P(),
        P(),
        P(),
        P(),
    )
    out_specs = P(("gx", "gy", "gz"), None)
    return jax.shard_map(
        per_device, mesh=mesh, in_specs=in_specs, out_specs=out_specs, check_vma=False
    )
```

```python
from functools import partial

import jax
import jax.numpy as jnp
from jax import lax
from jax.experimental import pallas as pl
from jax.experimental.pallas import tpu as pltpu
from jax.sharding import PartitionSpec as P

CX = 4
CY = 4
CZ = 4
PTS = 128
TERMS = 64
LEAF = CX * CY * CZ
EXT = (CX + 2) * (CY + 2) * (CZ + 2)
FEATS = 32
LINE = 8
PAIRS = 4
STEP = 16


SOFTEN = 0.0025
EXACT_DOTS = lax.Precision.HIGHEST


def iota(shape, dimension):
    return lax.broadcasted_iota(jnp.int32, shape, dimension)


def column(row):
    size = row.shape[1]
    eye = iota((size, size), 0) == iota((size, size), 1)
    return jnp.sum(jnp.where(eye, row, 0.0), axis=1, keepdims=True)


def over_plane(size_x, size_y, body, start, unroll=1):
    def line(x, carry):
        return lax.fori_loop(0, size_y, lambda y, held: body(x, y, held), carry, unroll=unroll)

    return lax.fori_loop(0, size_x, line, start)


def rounded(value):
    return value.astype(jnp.bfloat16).astype(jnp.float32)


def three_parts(value):
    high = rounded(value)
    middle = rounded(value - high)
    low = rounded(value - high - middle)
    return high, middle, low


def squares_of(points, shift_x, shift_y, shift_z, extra):
    row = iota((8, PTS), 0) % 4
    twice = jnp.concatenate([points, points], axis=0)
    place = twice + jnp.where(row == 0, shift_x, jnp.where(row == 1, shift_y, shift_z))
    square = place * place
    norm = square[0:1] + square[1:2] + square[2:3] + extra
    return jnp.where(row == 3, norm, place), row == 3, iota((8, PTS), 0) < 4


def source_features(points, shift_x, shift_y, shift_z):
    value, last, first = squares_of(points, shift_x, shift_y, shift_z, 0.0)
    high, middle, low = three_parts(value)
    scale = jnp.where(last, 1.0, -2.0)
    high_one = jnp.where(last, 1.0, -2.0 * high)
    middle_one = jnp.where(last, 1.0, -2.0 * middle)
    rows = [
        jnp.where(first, high * scale, middle * scale),
        jnp.where(first, low * scale, high_one),
        jnp.where(first, high_one, middle_one),
        jnp.zeros((8, PTS), jnp.float32),
    ]
    return jnp.concatenate(rows, axis=0).astype(jnp.bfloat16)


def target_features(points, shift_x, shift_y, shift_z):
    value, last, first = squares_of(points, shift_x, shift_y, shift_z, SOFTEN)
    high, middle, low = three_parts(value)
    high_one = jnp.where(last, 1.0, high)
    rows = [
        high_one,
        jnp.where(first, high_one, jnp.where(last, high, middle)),
        jnp.where(first, jnp.where(last, middle, low), jnp.where(last, low, middle)),
        jnp.zeros((8, PTS), jnp.float32),
    ]
    return jnp.transpose(jnp.concatenate(rows, axis=0)).astype(jnp.bfloat16)


def whole():
    return pl.BlockSpec(memory_space=pltpu.VMEM)


def scalars():
    return pl.BlockSpec(memory_space=pltpu.SMEM)


def anywhere():
    return pl.BlockSpec(memory_space=pl.ANY)


def axis_bits():
    low_bits = lax.axis_size("gz").bit_length() - 1
    mid_bits = lax.axis_size("gy").bit_length() - 1
    high_bits = lax.axis_size("gx").bit_length() - 1
    return (low_bits, mid_bits, high_bits)


SIDES = [
    (x, y, z)
    for x in (-1, 0, 1)
    for y in (-1, 0, 1)
    for z in (-1, 0, 1)
    if (x, y, z) != (0, 0, 0)
]


def rim(side, size, layers):
    if side > 0:
        return pl.ds(size, layers), pl.ds(0, layers)
    if side < 0:
        return pl.ds(layers, layers), pl.ds(size + layers, layers)
    return pl.ds(layers, size), pl.ds(layers, size)


def middle(cell):
    if isinstance(cell, int):
        return jnp.float32(cell) - (CX // 2 + 1)
    return cell.astype(jnp.float32) - (CX // 2 + 1)


def ext_index(x, y, z):
    return ((x + 1) * (CY + 2) + y + 1) * (CZ + 2) + z + 1


def clear_part(grouped, surface):
    def one(n, carry):
        grouped[n] = jnp.zeros((8, 16, 2 * TERMS), jnp.bfloat16)
        return carry

    lax.fori_loop(0, 64, one, 0)
    surface[...] = jnp.zeros((4, PTS), jnp.float32)


def upward_part(pos, charge, count, up, outer, masked, turned, wide_points, wide_dens, order_ref):
    row = count[...].astype(jnp.float32)
    counted = column(row)
    masked[...] = jnp.where(
        iota((LEAF, PTS), 1).astype(jnp.float32) < counted, charge[...], 0.0
    )
    spots = [jnp.broadcast_to(column(outer[c : c + 1, :]), (TERMS, PTS)) for c in range(3)]
    lanes = iota((TERMS, PTS), 1)

    def leaf(n, check):
        source = masked[pl.ds(n, 1), :]
        square = jnp.full((TERMS, PTS), SOFTEN, jnp.float32)
        for c in range(3):
            spread = spots[c] - pos[c, pl.ds(n, 1), :]
            square = square + spread * spread
        total = jnp.sum(lax.rsqrt(square) * source, axis=1, keepdims=True)
        return jnp.where(lanes == n, total, check)

    check = lax.fori_loop(0, LEAF, leaf, jnp.zeros((TERMS, PTS), jnp.float32), unroll=16)
    dens = jnp.dot(up[...], check, preferred_element_type=jnp.float32, precision=EXACT_DOTS)
    turned[...] = jnp.transpose(jnp.concatenate([dens, dens], axis=0))
    even = turned[pl.ds(0, LEAF // 2, stride=2), :]
    odd = turned[pl.ds(1, LEAF // 2, stride=2), :]
    both = jnp.where(iota((LEAF // 2, PTS), 1) < TERMS, even, odd)
    for m in range(LEAF // 2):
        x, y, z = m // (CY * CZ // 2), m // (CZ // 2) % CY, m % (CZ // 2)
        wide_dens[x + 2, y + 2, z + 1] = both[m : m + 1]
    return row, counted


def points_part(pos, masked, wide_points):
    def line(x, y, carry):
        for z in range(CZ):
            n = (x * CY + y) * CZ + z
            rows = [pos[c, pl.ds(n, 1), :] for c in range(3)] + [masked[pl.ds(n, 1), :]]
            wide_points[x + 1, y + 1, z + 1] = jnp.concatenate(rows, axis=0)
        return carry

    over_plane(CX, CY, line, 0, CY)


def order_part(row, counted, order_ref):
    leaf = iota((LEAF, LEAF), 0).astype(jnp.float32)
    other = iota((LEAF, LEAF), 1).astype(jnp.float32)
    mine = counted * LEAF + leaf
    theirs = row * LEAF + other
    rank = jnp.sum(jnp.where(theirs < mine, 1.0, 0.0), axis=1, keepdims=True)
    order = jnp.sum(jnp.where(rank == other, leaf, 0.0), axis=0, keepdims=True)
    order_ref[...] = jnp.concatenate([order, row], axis=1).astype(jnp.int32)


def weights_part(inner, weights):
    upper_lanes = iota((TERMS, 2 * TERMS), 1) >= TERMS
    spread = []
    for c in range(3):
        row = inner[c : c + 1, :]
        spread.append(jnp.concatenate([row, row], axis=1) - column(row))
    squares_z = []
    for pair in range(PAIRS):
        shift = jnp.where(upper_lanes, float(pair + 1), float(pair - 3))
        squares_z.append((spread[2] - shift) * (spread[2] - shift))

    def line(n_x, n_y, carry):
        shift_x = n_x - 3
        shift_y = n_y - 3
        d_x = spread[0] - shift_x.astype(jnp.float32)
        d_y = spread[1] - shift_y.astype(jnp.float32)
        plane = d_x * d_x + d_y * d_y + SOFTEN
        close = jnp.maximum(jnp.abs(shift_x), jnp.abs(shift_y)) < 2
        for pair in range(PAIRS):
            weight = lax.rsqrt(plane + squares_z[pair])
            if pair == 0:
                weight = jnp.where(close & upper_lanes, 0.0, weight)
            if pair >= 2:
                weight = jnp.where(close & ~upper_lanes, 0.0, weight)
            high = weight.astype(jnp.bfloat16)
            low = (weight - high.astype(jnp.float32)).astype(jnp.bfloat16)
            at = (n_x * 7 + n_y) * 2
            weights[at, pair * TERMS : (pair + 1) * TERMS] = high
            weights[at + 1, pair * TERMS : (pair + 1) * TERMS] = low
        return carry

    over_plane(7, 7, line, 0, 7)


def gather_part(wide_dens, raw, grouped):
    half = iota((8, 2 * TERMS), 1) < TERMS
    blank = jnp.zeros((8, 2 * TERMS), jnp.float32)

    def gather(a_x, a_y, carry):
        for b in range(3):
            for parent in range(8):
                cell_x = 2 * (parent // 4) + a_x
                cell_y = 2 * (parent // 2 % 2) + a_y
                raw[a_x * 18 + a_y * 3 + b, parent : parent + 1, :] = wide_dens[
                    cell_x, cell_y, parent % 2 + b
                ]
        return carry

    over_plane(6, 6, gather, 0, 6)

    def split(a_x, a_y, carry):
        whole_rows = []
        for b in range(3):
            value = raw[a_x * 18 + a_y * 3 + b]
            high = rounded(value)
            whole_rows.append((high, value - high))
        for part in range(2):
            first, second, third = (member[part] for member in whole_rows)
            one, two, three = (pltpu.roll(member, TERMS, 1) for member in (first, second, third))
            tiles = [
                (jnp.where(half, 0.0, one), first),
                (jnp.where(half, one, two), second),
                (jnp.where(half, two, three), third),
                (jnp.where(half, three, 0.0), blank),
            ]
            for at, rows in enumerate(tiles):
                grouped[(a_x + 1) * 8 + a_y + 1, 4 * part + at] = jnp.concatenate(
                    rows, axis=0
                ).astype(jnp.bfloat16)
        return carry

    over_plane(6, 6, split, 0, 6)


def translate_part(weights, grouped, down_ref, local):
    def product(places, parities):
        lefts = []
        rights = []
        for n_x, n_y in places:
            for lanes in range(2):
                pieces = []
                for kind in (0, 4, 2, 6):
                    for parity in parities:
                        at = (n_x + parity // 2) * 8 + n_y + parity % 2
                        pieces.append(grouped[at, kind + lanes])
                lefts.append(jnp.concatenate(pieces, axis=0))
            at = (n_x * 7 + n_y) * 2
            rights.append(jnp.concatenate([weights[at], weights[at + 1]], axis=1))
        result = jnp.dot(
            jnp.concatenate(lefts, axis=1),
            jnp.concatenate(rights, axis=0),
            preferred_element_type=jnp.float32,
        )
        for kind in range(4):
            for k, parity in enumerate(parities):
                at = (kind * len(parities) + k) * 16
                sums[kind * 4 + parity].append(result[at : at + 16])

    sums = [[] for _ in range(16)]
    inner_shifts = range(1, 6)
    product([(n_x, n_y) for n_x in inner_shifts for n_y in inner_shifts], (0, 1, 2, 3))
    product([(0, n_y) for n_y in range(7)], (2, 3))
    product([(6, n_y) for n_y in range(7)], (0, 1))
    product([(n_x, 0) for n_x in inner_shifts], (1, 3))
    product([(n_x, 6) for n_x in inner_shifts], (0, 2))
    total = jnp.concatenate([sum(rows[1:], rows[0]) for rows in sums], axis=0)
    total = total[:, : 2 * TERMS] + total[:, 2 * TERMS :]
    lower = total[:LEAF] + total[LEAF : 2 * LEAF]
    upper = total[2 * LEAF : 3 * LEAF] + total[3 * LEAF :]
    total = jnp.where(iota((LEAF, 2 * TERMS), 1) < TERMS, lower, upper)
    down = down_ref[...]
    down = jnp.concatenate([down, down], axis=1)
    down = jnp.concatenate([down, jnp.zeros_like(down)], axis=0)
    local[...] = lax.dot_general(
        total,
        down,
        (((1,), (1,)), ((), ())),
        preferred_element_type=jnp.float32,
        precision=EXACT_DOTS,
    )


def gather_body(
    pos_hbm,
    charge_hbm,
    count_hbm,
    up_hbm,
    down_hbm,
    inner_hbm,
    outer_hbm,
    wide_points,
    sources,
    targets,
    local,
    order_ref,
    wide_dens,
    pos,
    charge,
    count,
    up,
    down,
    inner,
    outer,
    masked,
    turned,
    weights,
    raw,
    grouped,
    surface,
    load_sem,
    send_sem,
    recv_sem,
):
    low_bits, mid_bits, high_bits = axis_bits()
    total_bits = low_bits + mid_bits + high_bits
    device = (
        lax.axis_index("gx") * 2**mid_bits + lax.axis_index("gy")
    ) * 2**low_bits + lax.axis_index("gz")
    place = []
    extent = []
    for c in range(3):
        bits = list(range(c, total_bits, 3))
        place.append(sum((device // 2**bit % 2) * 2**rank for rank, bit in enumerate(bits)))
        extent.append(2 ** len(bits))

    steps = []
    for c in range(3):
        moves = {}
        for move in (-1, 0, 1):
            moved = place[c] + move
            spot = [0, 0, 0]
            for rank, bit in enumerate(range(c, total_bits, 3)):
                digit = moved // 2**rank % 2
                if bit < low_bits:
                    spot[2] = spot[2] + digit * 2**bit
                elif bit < low_bits + mid_bits:
                    spot[1] = spot[1] + digit * 2 ** (bit - low_bits)
                else:
                    spot[0] = spot[0] + digit * 2 ** (bit - low_bits - mid_bits)
            moves[move] = spot
        steps.append(moves)
    room = [{1: place[c] < extent[c] - 1, -1: place[c] > 0} for c in range(3)]
    inside = {}
    for side in SIDES:
        held = None
        for c in range(3):
            if side[c] != 0:
                held = room[c][side[c]] if held is None else held & room[c][side[c]]
        inside[side] = held

    def there(side):
        return inside[side]

    def coordinates(side):
        return tuple(
            sum(steps[c][side[c]][axis] for c in range(3)) + jnp.int32(0) for axis in range(3)
        )

    kinds = (
        (wide_dens, (CX, CY, CZ // 2), (2, 2, 1)),
        (wide_points, (CX, CY, CZ), (1, 1, 1)),
    )

    def regions(kind, at):
        wide, sizes, layers = kinds[kind]
        return zip(*(rim(SIDES[at][c], sizes[c], layers[c]) for c in range(3)))

    def remote(kind, at):
        wide = kinds[kind][0]
        source, target = regions(kind, at)
        return pltpu.make_async_remote_copy(
            src_ref=wide.at[source],
            dst_ref=wide.at[target],
            send_sem=send_sem.at[kind, at],
            recv_sem=recv_sem.at[kind, at],
            device_id=coordinates(SIDES[at]),
            device_id_type=pl.DeviceIdType.MESH,
        )

    loads = [
        pltpu.make_async_copy(source, target, load_sem.at[at])
        for at, (source, target) in enumerate(
            (
                (pos_hbm, pos),
                (charge_hbm, charge),
                (count_hbm, count),
                (outer_hbm, outer),
                (up_hbm, up),
                (inner_hbm, inner),
                (down_hbm, down),
            )
        )
    ]
    for load in loads:
        load.start()
    barrier = pltpu.get_barrier_semaphore()
    met = jnp.int32(0)
    order = sorted(range(len(SIDES)), key=lambda at: -sum(map(abs, SIDES[at])))
    for at in order:
        met = met + jnp.where(there(SIDES[at]), 1, 0)

        @pl.when(there(SIDES[at]))
        def _(at=at):
            pl.semaphore_signal(
                barrier,
                inc=1,
                device_id=coordinates(SIDES[at]),
                device_id_type=pl.DeviceIdType.MESH,
            )

    clear_part(grouped, surface)
    for load in loads:
        load.wait()
    surface[0:3, 0:TERMS] = outer[...]
    row, counted = upward_part(
        pos, charge, count, up, outer, masked, turned, wide_points, wide_dens, order_ref
    )
    pl.semaphore_wait(barrier, met)

    def send(kind):
        for at in order:

            @pl.when(there(SIDES[at]))
            def _(at=at):
                remote(kind, at).start()

    def finish(kind):
        for at in order:

            @pl.when(there(SIDES[at]))
            def _(at=at):
                remote(kind, at).wait_send()

            @pl.when(there(tuple(-c for c in SIDES[at])))
            def _(at=at):
                remote(kind, at).wait_recv()

    def blank(kind):
        for at in order:

            @pl.when(~there(tuple(-c for c in SIDES[at])))
            def _(at=at):
                wide = kinds[kind][0]
                _, target = regions(kind, at)
                shape = tuple(piece.size for piece in target) + wide.shape[3:]
                wide[target] = jnp.zeros(shape, jnp.float32)

    send(0)
    points_part(pos, masked, wide_points)
    send(1)
    order_part(row, counted, order_ref)
    blank(0)
    blank(1)
    weights_part(inner, weights)

    def source(e_x, e_y, e_z):
        n = (e_x * (CY + 2) + e_y) * (CZ + 2) + e_z
        sources[n] = source_features(
            wide_points[e_x, e_y, e_z], middle(e_x), middle(e_y), middle(e_z)
        )

    def prepare_own(x, y, carry):
        for z in range(CZ):
            n = (x * CY + y) * CZ + z
            spot = (middle(x + 1), middle(y + 1), middle(z + 1))
            points = wide_points[x + 1, y + 1, z + 1]
            targets[n] = target_features(points, *spot)
            sources[ext_index(x, y, z)] = source_features(points, *spot)
            sources[EXT + n] = source_features(surface[...], *spot)
        return carry

    over_plane(CX, CY, prepare_own, 0, CY)
    finish(0)
    gather_part(wide_dens, raw, grouped)
    translate_part(weights, grouped, down, local)
    finish(1)

    def prepare_ends(y, carry):
        for e_x in (0, CX + 1):
            for e_z in range(CZ + 2):
                source(e_x, y, e_z)
        return carry

    def prepare_sides(x, carry):
        for e_y in (0, CY + 1):
            for e_z in range(CZ + 2):
                source(x, e_y, e_z)
        for e_y in range(1, CY + 1):
            for e_z in (0, CZ + 1):
                source(x, e_y, e_z)
        return carry

    lax.fori_loop(0, CY + 2, prepare_ends, 0)
    lax.fori_loop(1, CX + 1, prepare_sides, 0)


def near_body(order_ref, points_ref, sources, targets, local, out_ref, totals):
    lane = iota((1, PTS), 1)
    square_eye = iota((PTS, PTS), 0) == iota((PTS, PTS), 1)

    def rows(n, size):
        x, y, z = n >> 4, (n >> 2) & 3, n & 3
        base = ext_index(x, y, z)
        parity = (x & 1) * 4 + (y & 1) * 2 + (z & 1)
        parent = (x >> 1) * 4 + (y >> 1) * 2 + (z >> 1)
        blocks = []
        for s_x in range(-1, 2):
            for s_y in range(-1, 2):
                for s_z in range(-1, 2):
                    blocks.append(base + s_x * ((CY + 2) * (CZ + 2)) + s_y * (CZ + 2) + s_z)
        left = targets[n, 0:size, :]
        eye = iota((size, PTS), 0) == iota((size, PTS), 1)
        total = jnp.zeros((size, PTS), jnp.float32)
        for at in range(0, 28, 2):
            right = []
            charge = []
            for b in (at, at + 1):
                if b < 27:
                    right.append(sources[blocks[b]])
                    charge.append(points_ref[blocks[b], 3:4, :])
                else:
                    right.append(sources[EXT + n])
                    charge.append(local[pl.ds(parity * 8 + parent, 1), :])
            square = jnp.dot(
                left, jnp.concatenate(right, axis=1), preferred_element_type=jnp.float32
            )
            weight = lax.rsqrt(square)
            for k, b in enumerate((at, at + 1)):
                part = weight[:, k * PTS : (k + 1) * PTS]
                if b == 13:
                    part = jnp.where(eye, 0.0, part)
                total = total + part * charge[k]
        return total

    def finish(g):
        for k in range(LINE):
            n = order_ref[0, g * LINE + k]
            sums = jnp.sum(totals[k], axis=1, keepdims=True)
            flat = jnp.sum(jnp.where(square_eye, sums, 0.0), axis=0, keepdims=True)
            out_ref[pl.ds(n, 1), :] = jnp.where(lane < order_ref[0, LEAF + n], flat, 0.0)

    def leaf_group(g, carry):
        longest = order_ref[0, LEAF + order_ref[0, g * LINE + LINE - 1]]
        most = lax.div(longest + STEP - 1, STEP)

        def together(size):
            finish(jnp.maximum(g - 1, 0))
            for k in range(LINE):
                totals[k, 0:size, :] = rows(order_ref[0, g * LINE + k], size)

        def among(low, high):
            if high - low == 1:
                together(STEP * high)
                return
            mid = (low + high) // 2
            pl.when(most <= mid)(partial(among, low, mid))
            pl.when(most > mid)(partial(among, mid, high))

        among(0, PTS // STEP)
        return carry

    lax.fori_loop(0, LEAF // LINE, leaf_group, 0)
    finish(LEAF // LINE - 1)


def gather_all(positions, charges, counts, up_inverse, down_inverse, inner_surface, outer_surface):
    wide = (CX + 2, CY + 2, CZ + 2, 4, PTS)
    return pl.pallas_call(
        gather_body,
        out_shape=(
            pltpu.VMEM(wide, jnp.float32),
            pltpu.VMEM((EXT + LEAF, FEATS, PTS), jnp.bfloat16),
            pltpu.VMEM((LEAF, PTS, FEATS), jnp.bfloat16),
            pltpu.VMEM((LEAF, 2 * TERMS), jnp.float32),
            pltpu.VMEM((1, 2 * LEAF), jnp.int32),
        ),
        in_specs=[anywhere()] * 7,
        out_specs=(whole(),) * 5,
        scratch_shapes=[
            pltpu.VMEM((CX + 4, CY + 4, CZ // 2 + 2, 1, 2 * TERMS), jnp.float32),
            pltpu.VMEM((3, LEAF, PTS), jnp.float32),
            pltpu.VMEM((LEAF, PTS), jnp.float32),
            pltpu.VMEM((1, LEAF), jnp.int32),
            pltpu.VMEM((TERMS, TERMS), jnp.float32),
            pltpu.VMEM((TERMS, TERMS), jnp.float32),
            pltpu.VMEM((3, TERMS), jnp.float32),
            pltpu.VMEM((3, TERMS), jnp.float32),
            pltpu.VMEM((LEAF, PTS), jnp.float32),
            pltpu.VMEM((PTS, 2 * TERMS), jnp.float32),
            pltpu.VMEM((98, PAIRS * TERMS, 2 * TERMS), jnp.bfloat16),
            pltpu.VMEM((108, 8, 2 * TERMS), jnp.float32),
            pltpu.VMEM((64, 8, 16, 2 * TERMS), jnp.bfloat16),
            pltpu.VMEM((4, PTS), jnp.float32),
            pltpu.SemaphoreType.DMA((7,)),
            pltpu.SemaphoreType.DMA((2, len(SIDES))),
            pltpu.SemaphoreType.DMA((2, len(SIDES))),
        ],
        compiler_params=pltpu.CompilerParams(
            collective_id=0, has_side_effects=True, vmem_limit_bytes=32 * 2**20
        ),
        name="gather",
    )(positions, charges, counts, up_inverse, down_inverse, inner_surface, outer_surface)


def potentials(order, points, sources, targets, local):
    return pl.pallas_call(
        near_body,
        out_shape=jax.ShapeDtypeStruct((LEAF, PTS), jnp.float32),
        in_specs=[scalars()] + [whole()] * 4,
        out_specs=whole(),
        scratch_shapes=[pltpu.VMEM((LINE, PTS, PTS), jnp.float32)],
        compiler_params=pltpu.CompilerParams(vmem_limit_bytes=32 * 2**20),
        name="potentials",
    )(order, points, sources, targets, local)


def per_device(positions, charges, counts, up_inverse, down_inverse, inner_surface, outer_surface):
    arguments = (
        jnp.transpose(positions, (1, 0, 2)),
        charges,
        counts.reshape(1, LEAF),
        up_inverse,
        down_inverse,
        inner_surface,
        outer_surface,
    )
    points, sources, targets, local, order = gather_all(
        *(pltpu.with_memory_space_constraint(member, pltpu.HBM) for member in arguments)
    )
    return potentials(order, points.reshape(EXT, 4, PTS), sources, targets, local)


def solution(mesh):
    in_specs = (
        P(("gx", "gy", "gz"), None, None),
        P(("gx", "gy", "gz"), None),
        P(("gx", "gy", "gz")),
        P(),
        P(),
        P(),
        P(),
    )
    out_specs = P(("gx", "gy", "gz"), None)
    return jax.shard_map(
        per_device, mesh=mesh, in_specs=in_specs, out_specs=out_specs, check_vma=False
    )
```

```python
from functools import partial

import jax
import jax.numpy as jnp
from jax import lax
from jax.experimental import pallas as pl
from jax.experimental.pallas import tpu as pltpu
from jax.sharding import PartitionSpec as P

CX = 4
CY = 4
CZ = 4
PTS = 128
TERMS = 64
LEAF = CX * CY * CZ
EXT = (CX + 2) * (CY + 2) * (CZ + 2)
FEATS = 32
LINE = 8
PAIRS = 4
STEP = 16


SOFTEN = 0.0025
EXACT_DOTS = lax.Precision.HIGHEST


def iota(shape, dimension):
    return lax.broadcasted_iota(jnp.int32, shape, dimension)


def column(row):
    size = row.shape[1]
    eye = iota((size, size), 0) == iota((size, size), 1)
    return jnp.sum(jnp.where(eye, row, 0.0), axis=1, keepdims=True)


def over_plane(size_x, size_y, body, start, unroll=1):
    def line(x, carry):
        return lax.fori_loop(0, size_y, lambda y, held: body(x, y, held), carry, unroll=unroll)

    return lax.fori_loop(0, size_x, line, start)


def rounded(value):
    return value.astype(jnp.bfloat16).astype(jnp.float32)


def three_parts(value):
    high = rounded(value)
    middle = rounded(value - high)
    low = rounded(value - high - middle)
    return high, middle, low


def squares_of(points, shift_x, shift_y, shift_z, extra):
    row = iota((8, PTS), 0) % 4
    twice = jnp.concatenate([points, points], axis=0)
    place = twice + jnp.where(row == 0, shift_x, jnp.where(row == 1, shift_y, shift_z))
    square = place * place
    norm = square[0:1] + square[1:2] + square[2:3] + extra
    return jnp.where(row == 3, norm, place), row == 3, iota((8, PTS), 0) < 4


def source_features(points, spots):
    row = iota((8, PTS), 0)
    last, first = row % 4 == 3, row < 4
    both = jnp.concatenate(points, axis=0)
    shift = jnp.where(first, spots[0][2], spots[1][2])
    shift = jnp.where(row % 4 == 0, jnp.where(first, spots[0][0], spots[1][0]), shift)
    shift = jnp.where(row % 4 == 1, jnp.where(first, spots[0][1], spots[1][1]), shift)
    place = both + shift
    square = place * place
    norm = pltpu.roll(square, 1, 0) + pltpu.roll(square, 2, 0) + pltpu.roll(square, 3, 0)
    high, middle, low = three_parts(jnp.where(last, norm, -2.0 * place))
    high_one = jnp.where(last, 1.0, high)
    middle_one = jnp.where(last, 1.0, middle)
    pairs = ((high, middle), (low, high_one), (high_one, middle_one))
    blank = jnp.zeros((8, PTS), jnp.float32)
    lower = [jnp.where(first, one, pltpu.roll(two, 4, 0)) for one, two in pairs]
    upper = [jnp.where(first, pltpu.roll(one, 4, 0), two) for one, two in pairs]
    return [
        jnp.concatenate(rows + [blank], axis=0).astype(jnp.bfloat16) for rows in (lower, upper)
    ]


def target_features(points, shift_x, shift_y, shift_z):
    value, last, first = squares_of(points, shift_x, shift_y, shift_z, SOFTEN)
    high, middle, low = three_parts(value)
    high_one = jnp.where(last, 1.0, high)
    rows = [
        high_one,
        jnp.where(first, high_one, jnp.where(last, high, middle)),
        jnp.where(first, jnp.where(last, middle, low), jnp.where(last, low, middle)),
        jnp.zeros((8, PTS), jnp.float32),
    ]
    return jnp.transpose(jnp.concatenate(rows, axis=0)).astype(jnp.bfloat16)


def whole():
    return pl.BlockSpec(memory_space=pltpu.VMEM)


def scalars():
    return pl.BlockSpec(memory_space=pltpu.SMEM)


def anywhere():
    return pl.BlockSpec(memory_space=pl.ANY)


def axis_bits():
    low_bits = lax.axis_size("gz").bit_length() - 1
    mid_bits = lax.axis_size("gy").bit_length() - 1
    high_bits = lax.axis_size("gx").bit_length() - 1
    return (low_bits, mid_bits, high_bits)


SIDES = [
    (x, y, z)
    for x in (-1, 0, 1)
    for y in (-1, 0, 1)
    for z in (-1, 0, 1)
    if (x, y, z) != (0, 0, 0)
]


def rim(side, size, layers):
    if side > 0:
        return pl.ds(size, layers), pl.ds(0, layers)
    if side < 0:
        return pl.ds(layers, layers), pl.ds(size + layers, layers)
    return pl.ds(layers, size), pl.ds(layers, size)


def middle(cell):
    if isinstance(cell, int):
        return jnp.float32(cell) - (CX // 2 + 1)
    return cell.astype(jnp.float32) - (CX // 2 + 1)


def ext_index(x, y, z):
    return ((x + 1) * (CY + 2) + y + 1) * (CZ + 2) + z + 1


def clear_part(grouped, surface):
    def one(n, carry):
        grouped[n] = jnp.zeros((8, 16, 2 * TERMS), jnp.bfloat16)
        return carry

    lax.fori_loop(0, 64, one, 0)
    surface[...] = jnp.zeros((4, PTS), jnp.float32)


def upward_part(pos, charge, count, up, outer, masked, turned, wide_points, wide_dens, order_ref):
    row = count[...].astype(jnp.float32)
    counted = column(row)
    masked[...] = jnp.where(
        iota((LEAF, PTS), 1).astype(jnp.float32) < counted, charge[...], 0.0
    )
    spots = [jnp.broadcast_to(column(outer[c : c + 1, :]), (TERMS, PTS)) for c in range(3)]
    lanes = iota((TERMS, PTS), 1)

    def leaf(n, check):
        source = masked[pl.ds(n, 1), :]
        square = jnp.full((TERMS, PTS), SOFTEN, jnp.float32)
        for c in range(3):
            spread = spots[c] - pos[c, pl.ds(n, 1), :]
            square = square + spread * spread
        total = jnp.sum(lax.rsqrt(square) * source, axis=1, keepdims=True)
        return jnp.where(lanes == n, total, check)

    check = lax.fori_loop(0, LEAF, leaf, jnp.zeros((TERMS, PTS), jnp.float32), unroll=16)
    dens = jnp.dot(up[...], check, preferred_element_type=jnp.float32, precision=EXACT_DOTS)
    turned[...] = jnp.transpose(jnp.concatenate([dens, dens], axis=0))
    even = turned[pl.ds(0, LEAF // 2, stride=2), :]
    odd = turned[pl.ds(1, LEAF // 2, stride=2), :]
    both = jnp.where(iota((LEAF // 2, PTS), 1) < TERMS, even, odd)
    for m in range(LEAF // 2):
        x, y, z = m // (CY * CZ // 2), m // (CZ // 2) % CY, m % (CZ // 2)
        wide_dens[x + 2, y + 2, z + 1] = both[m : m + 1]
    return row, counted


def points_part(pos, masked, wide_points):
    def line(x, y, carry):
        for z in range(CZ):
            n = (x * CY + y) * CZ + z
            rows = [pos[c, pl.ds(n, 1), :] for c in range(3)] + [masked[pl.ds(n, 1), :]]
            wide_points[x + 1, y + 1, z + 1] = jnp.concatenate(rows, axis=0)
        return carry

    over_plane(CX, CY, line, 0, CY)


def order_part(row, counted, order_ref):
    leaf = iota((LEAF, LEAF), 0).astype(jnp.float32)
    other = iota((LEAF, LEAF), 1).astype(jnp.float32)
    mine = counted * LEAF + leaf
    theirs = row * LEAF + other
    rank = jnp.sum(jnp.where(theirs < mine, 1.0, 0.0), axis=1, keepdims=True)
    order = jnp.sum(jnp.where(rank == other, leaf, 0.0), axis=0, keepdims=True)
    order_ref[...] = jnp.concatenate([order, row], axis=1).astype(jnp.int32)


def weights_part(inner, weights):
    upper_lanes = iota((TERMS, 2 * TERMS), 1) >= TERMS
    spread = []
    for c in range(3):
        row = inner[c : c + 1, :]
        spread.append(jnp.concatenate([row, row], axis=1) - column(row))
    squares_z = []
    for pair in range(PAIRS):
        shift = jnp.where(upper_lanes, float(pair + 1), float(pair - 3))
        squares_z.append((spread[2] - shift) * (spread[2] - shift))

    def line(n_x, n_y, carry):
        shift_x = n_x - 3
        shift_y = n_y - 3
        d_x = spread[0] - shift_x.astype(jnp.float32)
        d_y = spread[1] - shift_y.astype(jnp.float32)
        plane = d_x * d_x + d_y * d_y + SOFTEN
        close = jnp.maximum(jnp.abs(shift_x), jnp.abs(shift_y)) < 2
        for pair in range(PAIRS):
            weight = lax.rsqrt(plane + squares_z[pair])
            if pair == 0:
                weight = jnp.where(close & upper_lanes, 0.0, weight)
            if pair >= 2:
                weight = jnp.where(close & ~upper_lanes, 0.0, weight)
            high = weight.astype(jnp.bfloat16)
            low = (weight - high.astype(jnp.float32)).astype(jnp.bfloat16)
            at = (n_x * 7 + n_y) * 2
            weights[at, pair * TERMS : (pair + 1) * TERMS] = high
            weights[at + 1, pair * TERMS : (pair + 1) * TERMS] = low
        return carry

    over_plane(7, 7, line, 0, 7)


def gather_part(wide_dens, raw, grouped):
    half = iota((8, 2 * TERMS), 1) < TERMS
    blank = jnp.zeros((8, 2 * TERMS), jnp.float32)

    def gather(a_x, a_y, carry):
        for b in range(3):
            for parent in range(8):
                cell_x = 2 * (parent // 4) + a_x
                cell_y = 2 * (parent // 2 % 2) + a_y
                raw[a_x * 18 + a_y * 3 + b, parent : parent + 1, :] = wide_dens[
                    cell_x, cell_y, parent % 2 + b
                ]
        return carry

    over_plane(6, 6, gather, 0, 6)

    def split(a_x, a_y, carry):
        whole_rows = []
        for b in range(3):
            value = raw[a_x * 18 + a_y * 3 + b]
            high = rounded(value)
            whole_rows.append((high, value - high))
        for part in range(2):
            first, second, third = (member[part] for member in whole_rows)
            one, two, three = (pltpu.roll(member, TERMS, 1) for member in (first, second, third))
            tiles = [
                (jnp.where(half, 0.0, one), first),
                (jnp.where(half, one, two), second),
                (jnp.where(half, two, three), third),
                (jnp.where(half, three, 0.0), blank),
            ]
            for at, rows in enumerate(tiles):
                grouped[(a_x + 1) * 8 + a_y + 1, 4 * part + at] = jnp.concatenate(
                    rows, axis=0
                ).astype(jnp.bfloat16)
        return carry

    over_plane(6, 6, split, 0, 6)


def translate_part(weights, grouped, down_ref, local):
    def product(places, parities):
        lefts = []
        rights = []
        for n_x, n_y in places:
            for lanes in range(2):
                pieces = []
                for kind in (0, 4, 2, 6):
                    for parity in parities:
                        at = (n_x + parity // 2) * 8 + n_y + parity % 2
                        pieces.append(grouped[at, kind + lanes])
                lefts.append(jnp.concatenate(pieces, axis=0))
            at = (n_x * 7 + n_y) * 2
            rights.append(jnp.concatenate([weights[at], weights[at + 1]], axis=1))
        result = jnp.dot(
            jnp.concatenate(lefts, axis=1),
            jnp.concatenate(rights, axis=0),
            preferred_element_type=jnp.float32,
        )
        for kind in range(4):
            for k, parity in enumerate(parities):
                at = (kind * len(parities) + k) * 16
                sums[kind * 4 + parity].append(result[at : at + 16])

    sums = [[] for _ in range(16)]
    inner_shifts = range(1, 6)
    product([(n_x, n_y) for n_x in inner_shifts for n_y in inner_shifts], (0, 1, 2, 3))
    product([(0, n_y) for n_y in range(7)], (2, 3))
    product([(6, n_y) for n_y in range(7)], (0, 1))
    product([(n_x, 0) for n_x in inner_shifts], (1, 3))
    product([(n_x, 6) for n_x in inner_shifts], (0, 2))
    total = jnp.concatenate([sum(rows[1:], rows[0]) for rows in sums], axis=0)
    total = total[:, : 2 * TERMS] + total[:, 2 * TERMS :]
    lower = total[:LEAF] + total[LEAF : 2 * LEAF]
    upper = total[2 * LEAF : 3 * LEAF] + total[3 * LEAF :]
    total = jnp.where(iota((LEAF, 2 * TERMS), 1) < TERMS, lower, upper)
    down = down_ref[...]
    down = jnp.concatenate([down, down], axis=1)
    down = jnp.concatenate([down, jnp.zeros_like(down)], axis=0)
    local[...] = lax.dot_general(
        total,
        down,
        (((1,), (1,)), ((), ())),
        preferred_element_type=jnp.float32,
        precision=EXACT_DOTS,
    )


def gather_body(
    pos_hbm,
    charge_hbm,
    count_hbm,
    up_hbm,
    down_hbm,
    inner_hbm,
    outer_hbm,
    wide_points,
    sources,
    targets,
    local,
    order_ref,
    wide_dens,
    pos,
    charge,
    count,
    up,
    down,
    inner,
    outer,
    masked,
    turned,
    weights,
    raw,
    grouped,
    surface,
    order_rows,
    load_sem,
    send_sem,
    recv_sem,
):
    low_bits, mid_bits, high_bits = axis_bits()
    total_bits = low_bits + mid_bits + high_bits
    device = (
        lax.axis_index("gx") * 2**mid_bits + lax.axis_index("gy")
    ) * 2**low_bits + lax.axis_index("gz")
    place = []
    extent = []
    for c in range(3):
        bits = list(range(c, total_bits, 3))
        place.append(sum(((device >> bit) & 1) * 2**rank for rank, bit in enumerate(bits)))
        extent.append(2 ** len(bits))

    steps = []
    for c in range(3):
        moves = {}
        for move in (-1, 0, 1):
            moved = place[c] + move
            spot = [0, 0, 0]
            for rank, bit in enumerate(range(c, total_bits, 3)):
                digit = (moved >> rank) & 1
                if bit < low_bits:
                    spot[2] = spot[2] + digit * 2**bit
                elif bit < low_bits + mid_bits:
                    spot[1] = spot[1] + digit * 2 ** (bit - low_bits)
                else:
                    spot[0] = spot[0] + digit * 2 ** (bit - low_bits - mid_bits)
            moves[move] = spot
        steps.append(moves)
    room = [{1: place[c] < extent[c] - 1, -1: place[c] > 0} for c in range(3)]
    inside = {}
    for side in SIDES:
        held = None
        for c in range(3):
            if side[c] != 0:
                held = room[c][side[c]] if held is None else held & room[c][side[c]]
        inside[side] = held

    def there(side):
        return inside[side]

    def coordinates(side):
        return tuple(
            sum(steps[c][side[c]][axis] for c in range(3)) + jnp.int32(0) for axis in range(3)
        )

    kinds = (
        (wide_dens, (CX, CY, CZ // 2), (2, 2, 1)),
        (wide_points, (CX, CY, CZ), (1, 1, 1)),
    )

    def regions(kind, at):
        wide, sizes, layers = kinds[kind]
        return zip(*(rim(SIDES[at][c], sizes[c], layers[c]) for c in range(3)))

    def remote(kind, at):
        wide = kinds[kind][0]
        source, target = regions(kind, at)
        return pltpu.make_async_remote_copy(
            src_ref=wide.at[source],
            dst_ref=wide.at[target],
            send_sem=send_sem.at[kind, at],
            recv_sem=recv_sem.at[kind, at],
            device_id=coordinates(SIDES[at]),
            device_id_type=pl.DeviceIdType.MESH,
        )

    loads = [
        pltpu.make_async_copy(source, target, load_sem.at[at])
        for at, (source, target) in enumerate(
            (
                (pos_hbm, pos),
                (charge_hbm, charge),
                (count_hbm, count),
                (outer_hbm, outer),
                (up_hbm, up),
                (inner_hbm, inner),
                (down_hbm, down),
            )
        )
    ]
    for load in loads:
        load.start()
    barrier = pltpu.get_barrier_semaphore()
    met = jnp.int32(0)
    order = sorted(range(len(SIDES)), key=lambda at: -sum(map(abs, SIDES[at])))
    for at in order:
        met = met + jnp.where(there(SIDES[at]), 1, 0)

        @pl.when(there(SIDES[at]))
        def _(at=at):
            pl.semaphore_signal(
                barrier,
                inc=1,
                device_id=coordinates(SIDES[at]),
                device_id_type=pl.DeviceIdType.MESH,
            )

    clear_part(grouped, surface)
    for load in loads:
        load.wait()
    surface[0:3, 0:TERMS] = outer[...]
    row, counted = upward_part(
        pos, charge, count, up, outer, masked, turned, wide_points, wide_dens, order_ref
    )
    pl.semaphore_wait(barrier, met)

    def send(kind):
        for at in order:

            @pl.when(there(SIDES[at]))
            def _(at=at):
                remote(kind, at).start()

    def finish(kind):
        for at in order:

            @pl.when(there(SIDES[at]))
            def _(at=at):
                remote(kind, at).wait_send()

            @pl.when(there(tuple(-c for c in SIDES[at])))
            def _(at=at):
                remote(kind, at).wait_recv()

    def blank(kind):
        for at in order:

            @pl.when(~there(tuple(-c for c in SIDES[at])))
            def _(at=at):
                wide = kinds[kind][0]
                _, target = regions(kind, at)
                shape = tuple(piece.size for piece in target) + wide.shape[3:]
                wide[target] = jnp.zeros(shape, jnp.float32)

    send(0)
    points_part(pos, masked, wide_points)
    send(1)
    order_part(row, counted, order_rows)
    ordering = pltpu.make_async_copy(order_rows, order_ref, load_sem.at[7])
    ordering.start()
    blank(0)
    blank(1)
    weights_part(inner, weights)

    def source(e_x, e_y, e_z, other):
        base = (e_x * (CY + 2) + e_y) * (CZ + 2)
        made = source_features(
            [wide_points[e_x, e_y, at] for at in (e_z, other)],
            [(middle(e_x), middle(e_y), middle(at)) for at in (e_z, other)],
        )
        for at, features in zip((e_z, other), made):
            sources[base + at] = features

    def prepare_own(x, y, carry):
        for z in range(0, CZ, 2):
            source(x + 1, y + 1, z + 1, z + 2)
            n = (x * CY + y) * CZ + z
            spots = [(middle(x + 1), middle(y + 1), middle(z + k + 1)) for k in range(2)]
            for k, features in enumerate(source_features([surface[...]] * 2, spots)):
                sources[EXT + n + k] = features
            for k in range(2):
                points = wide_points[x + 1, y + 1, z + k + 1]
                targets[n + k] = target_features(points, *spots[k])
        return carry

    over_plane(CX, CY, prepare_own, 0, CY)
    ordering.wait()
    finish(0)
    gather_part(wide_dens, raw, grouped)
    translate_part(weights, grouped, down, local)
    finish(1)

    def prepare_ends(y, carry):
        for e_x in (0, CX + 1):
            for e_z in range(0, CZ + 2, 2):
                source(e_x, y, e_z, e_z + 1)
        return carry

    def prepare_sides(x, carry):
        for e_y in (0, CY + 1):
            for e_z in range(0, CZ + 2, 2):
                source(x, e_y, e_z, e_z + 1)
        for e_y in range(1, CY + 1):
            source(x, e_y, 0, CZ + 1)
        return carry

    lax.fori_loop(0, CY + 2, prepare_ends, 0)
    lax.fori_loop(1, CX + 1, prepare_sides, 0)


def near_body(order_ref, points_ref, sources, targets, local, out_ref, totals):
    lane = iota((1, PTS), 1)
    square_eye = iota((PTS, PTS), 0) == iota((PTS, PTS), 1)

    def rows(n, size):
        x, y, z = n >> 4, (n >> 2) & 3, n & 3
        base = ext_index(x, y, z)
        parity = (x & 1) * 4 + (y & 1) * 2 + (z & 1)
        parent = (x >> 1) * 4 + (y >> 1) * 2 + (z >> 1)
        blocks = []
        for s_x in range(-1, 2):
            for s_y in range(-1, 2):
                for s_z in range(-1, 2):
                    blocks.append(base + s_x * ((CY + 2) * (CZ + 2)) + s_y * (CZ + 2) + s_z)
        left = targets[n, 0:size, :]
        eye = iota((size, PTS), 0) == iota((size, PTS), 1)
        total = jnp.zeros((size, PTS), jnp.float32)
        for at in range(0, 28, 2):
            right = []
            charge = []
            for b in (at, at + 1):
                if b < 27:
                    right.append(sources[blocks[b]])
                    charge.append(points_ref[blocks[b], 3:4, :])
                else:
                    right.append(sources[EXT + n])
                    charge.append(local[pl.ds(parity * 8 + parent, 1), :])
            square = jnp.dot(
                left, jnp.concatenate(right, axis=1), preferred_element_type=jnp.float32
            )
            weight = lax.rsqrt(square)
            for k, b in enumerate((at, at + 1)):
                part = weight[:, k * PTS : (k + 1) * PTS]
                if b == 13:
                    part = jnp.where(eye, 0.0, part)
                total = total + part * charge[k]
        return total

    def finish(g):
        for k in range(LINE):
            n = order_ref[0, g * LINE + k]
            sums = jnp.sum(totals[k], axis=1, keepdims=True)
            flat = jnp.sum(jnp.where(square_eye, sums, 0.0), axis=0, keepdims=True)
            out_ref[pl.ds(n, 1), :] = jnp.where(lane < order_ref[0, LEAF + n], flat, 0.0)

    def leaf_group(g, carry):
        def steps_of(k):
            return lax.div(order_ref[0, LEAF + order_ref[0, g * LINE + k]] + STEP - 1, STEP)

        most = steps_of(LINE - 1)
        alike = steps_of(LINE // 2 - 1) == most

        def together(lower, upper):
            finish(jnp.maximum(g - 1, 0))
            for k in range(LINE):
                size = lower if k < LINE // 2 else upper
                totals[k, 0:size, :] = rows(order_ref[0, g * LINE + k], size)

        def among(low, high):
            if high - low == 1:
                size = STEP * high
                if low == 0:
                    together(size, size)
                else:
                    pl.when(alike)(partial(together, size, size))
                    pl.when(~alike)(partial(together, size - STEP, size))
                return
            mid = (low + high) // 2
            pl.when(most <= mid)(partial(among, low, mid))
            pl.when(most > mid)(partial(among, mid, high))

        among(0, PTS // STEP)
        return carry

    lax.fori_loop(0, LEAF // LINE, leaf_group, 0)
    finish(LEAF // LINE - 1)


def gather_all(positions, charges, counts, up_inverse, down_inverse, inner_surface, outer_surface):
    wide = (CX + 2, CY + 2, CZ + 2, 4, PTS)
    return pl.pallas_call(
        gather_body,
        out_shape=(
            pltpu.VMEM(wide, jnp.float32),
            pltpu.VMEM((EXT + LEAF, FEATS, PTS), jnp.bfloat16),
            pltpu.VMEM((LEAF, PTS, FEATS), jnp.bfloat16),
            pltpu.VMEM((LEAF, 2 * TERMS), jnp.float32),
            pltpu.SMEM((1, 2 * LEAF), jnp.int32),
        ),
        in_specs=[anywhere()] * 7,
        out_specs=(whole(),) * 4 + (scalars(),),
        scratch_shapes=[
            pltpu.VMEM((CX + 4, CY + 4, CZ // 2 + 2, 1, 2 * TERMS), jnp.float32),
            pltpu.VMEM((3, LEAF, PTS), jnp.float32),
            pltpu.VMEM((LEAF, PTS), jnp.float32),
            pltpu.VMEM((1, LEAF), jnp.int32),
            pltpu.VMEM((TERMS, TERMS), jnp.float32),
            pltpu.VMEM((TERMS, TERMS), jnp.float32),
            pltpu.VMEM((3, TERMS), jnp.float32),
            pltpu.VMEM((3, TERMS), jnp.float32),
            pltpu.VMEM((LEAF, PTS), jnp.float32),
            pltpu.VMEM((PTS, 2 * TERMS), jnp.float32),
            pltpu.VMEM((98, PAIRS * TERMS, 2 * TERMS), jnp.bfloat16),
            pltpu.VMEM((108, 8, 2 * TERMS), jnp.float32),
            pltpu.VMEM((64, 8, 16, 2 * TERMS), jnp.bfloat16),
            pltpu.VMEM((4, PTS), jnp.float32),
            pltpu.VMEM((1, 2 * LEAF), jnp.int32),
            pltpu.SemaphoreType.DMA((8,)),
            pltpu.SemaphoreType.DMA((2, len(SIDES))),
            pltpu.SemaphoreType.DMA((2, len(SIDES))),
        ],
        compiler_params=pltpu.CompilerParams(
            collective_id=0, has_side_effects=True, vmem_limit_bytes=32 * 2**20
        ),
        name="gather",
    )(positions, charges, counts, up_inverse, down_inverse, inner_surface, outer_surface)


def potentials(order, points, sources, targets, local):
    return pl.pallas_call(
        near_body,
        out_shape=jax.ShapeDtypeStruct((LEAF, PTS), jnp.float32),
        in_specs=[scalars()] + [whole()] * 4,
        out_specs=whole(),
        scratch_shapes=[pltpu.VMEM((LINE, PTS, PTS), jnp.float32)],
        compiler_params=pltpu.CompilerParams(vmem_limit_bytes=32 * 2**20),
        name="potentials",
    )(order, points, sources, targets, local)


def per_device(positions, charges, counts, up_inverse, down_inverse, inner_surface, outer_surface):
    arguments = (
        jnp.transpose(positions, (1, 0, 2)),
        charges,
        counts.reshape(1, LEAF),
        up_inverse,
        down_inverse,
        inner_surface,
        outer_surface,
    )
    points, sources, targets, local, order = gather_all(
        *(pltpu.with_memory_space_constraint(member, pltpu.HBM) for member in arguments)
    )
    return potentials(order, points.reshape(EXT, 4, PTS), sources, targets, local)


def solution(mesh):
    in_specs = (
        P(("gx", "gy", "gz"), None, None),
        P(("gx", "gy", "gz"), None),
        P(("gx", "gy", "gz")),
        P(),
        P(),
        P(),
        P(),
    )
    out_specs = P(("gx", "gy", "gz"), None)
    return jax.shard_map(
        per_device, mesh=mesh, in_specs=in_specs, out_specs=out_specs, check_vma=False
    )
```

```python
from functools import partial

import jax
import jax.numpy as jnp
from jax import lax
from jax.experimental import pallas as pl
from jax.experimental.pallas import tpu as pltpu
from jax.sharding import PartitionSpec as P

CX = 4
CY = 4
CZ = 4
PTS = 128
TERMS = 64
LEAF = CX * CY * CZ
EXT = (CX + 2) * (CY + 2) * (CZ + 2)
FEATS = 32
LINE = 8
PAIRS = 4
STEP = 16


SOFTEN = 0.0025
EXACT_DOTS = lax.Precision.HIGHEST


def iota(shape, dimension):
    return lax.broadcasted_iota(jnp.int32, shape, dimension)


def column(row):
    size = row.shape[1]
    eye = iota((size, size), 0) == iota((size, size), 1)
    return jnp.sum(jnp.where(eye, row, 0.0), axis=1, keepdims=True)


def over_plane(size_x, size_y, body, start, unroll=1):
    def line(x, carry):
        return lax.fori_loop(0, size_y, lambda y, held: body(x, y, held), carry, unroll=unroll)

    return lax.fori_loop(0, size_x, line, start)


def rounded(value):
    return value.astype(jnp.bfloat16).astype(jnp.float32)


def three_parts(value):
    high = rounded(value)
    middle = rounded(value - high)
    low = rounded(value - high - middle)
    return high, middle, low


def squares_of(points, shift_x, shift_y, shift_z, extra):
    row = iota((8, PTS), 0) % 4
    twice = jnp.concatenate([points, points], axis=0)
    place = twice + jnp.where(row == 0, shift_x, jnp.where(row == 1, shift_y, shift_z))
    square = place * place
    norm = square[0:1] + square[1:2] + square[2:3] + extra
    return jnp.where(row == 3, norm, place), row == 3, iota((8, PTS), 0) < 4


def source_features(points, spots):
    row = iota((8, PTS), 0)
    last, first = row % 4 == 3, row < 4
    both = jnp.concatenate(points, axis=0)
    shift = jnp.where(first, spots[0][2], spots[1][2])
    shift = jnp.where(row % 4 == 0, jnp.where(first, spots[0][0], spots[1][0]), shift)
    shift = jnp.where(row % 4 == 1, jnp.where(first, spots[0][1], spots[1][1]), shift)
    place = both + shift
    square = place * place
    norm = pltpu.roll(square, 1, 0) + pltpu.roll(square, 2, 0) + pltpu.roll(square, 3, 0)
    high, middle, low = three_parts(jnp.where(last, norm, -2.0 * place))
    high_one = jnp.where(last, 1.0, high)
    middle_one = jnp.where(last, 1.0, middle)
    pairs = ((high, middle), (low, high_one), (high_one, middle_one))
    blank = jnp.zeros((8, PTS), jnp.float32)
    lower = [jnp.where(first, one, pltpu.roll(two, 4, 0)) for one, two in pairs]
    upper = [jnp.where(first, pltpu.roll(one, 4, 0), two) for one, two in pairs]
    return [
        jnp.concatenate(rows + [blank], axis=0).astype(jnp.bfloat16) for rows in (lower, upper)
    ]


def target_features(points, shift_x, shift_y, shift_z):
    value, last, first = squares_of(points, shift_x, shift_y, shift_z, SOFTEN)
    high, middle, low = three_parts(value)
    high_one = jnp.where(last, 1.0, high)
    rows = [
        high_one,
        jnp.where(first, high_one, jnp.where(last, high, middle)),
        jnp.where(first, jnp.where(last, middle, low), jnp.where(last, low, middle)),
        jnp.zeros((8, PTS), jnp.float32),
    ]
    return jnp.transpose(jnp.concatenate(rows, axis=0)).astype(jnp.bfloat16)


def whole():
    return pl.BlockSpec(memory_space=pltpu.VMEM)


def scalars():
    return pl.BlockSpec(memory_space=pltpu.SMEM)


def anywhere():
    return pl.BlockSpec(memory_space=pl.ANY)


def axis_bits():
    low_bits = lax.axis_size("gz").bit_length() - 1
    mid_bits = lax.axis_size("gy").bit_length() - 1
    high_bits = lax.axis_size("gx").bit_length() - 1
    return (low_bits, mid_bits, high_bits)


SIDES = [
    (x, y, z)
    for x in (-1, 0, 1)
    for y in (-1, 0, 1)
    for z in (-1, 0, 1)
    if (x, y, z) != (0, 0, 0)
]


def rim(side, size, layers):
    if side > 0:
        return pl.ds(size, layers), pl.ds(0, layers)
    if side < 0:
        return pl.ds(layers, layers), pl.ds(size + layers, layers)
    return pl.ds(layers, size), pl.ds(layers, size)


def middle(cell):
    if isinstance(cell, int):
        return jnp.float32(cell) - (CX // 2 + 1)
    return cell.astype(jnp.float32) - (CX // 2 + 1)


def ext_index(x, y, z):
    return ((x + 1) * (CY + 2) + y + 1) * (CZ + 2) + z + 1


def clear_part(grouped, surface):
    def one(n, carry):
        grouped[n] = jnp.zeros((8, 16, 2 * TERMS), jnp.bfloat16)
        return carry

    lax.fori_loop(0, 64, one, 0)
    surface[...] = jnp.zeros((4, PTS), jnp.float32)


def upward_part(pos, charge, count, up, outer, masked, turned, wide_points, wide_dens, order_ref):
    row = count[...].astype(jnp.float32)
    counted = column(row)
    masked[...] = jnp.where(
        iota((LEAF, PTS), 1).astype(jnp.float32) < counted, charge[...], 0.0
    )
    spots = [jnp.broadcast_to(column(outer[c : c + 1, :]), (TERMS, PTS)) for c in range(3)]
    lanes = iota((TERMS, PTS), 1)

    def leaf(n, check):
        source = masked[pl.ds(n, 1), :]
        square = jnp.full((TERMS, PTS), SOFTEN, jnp.float32)
        for c in range(3):
            spread = spots[c] - pos[c, pl.ds(n, 1), :]
            square = square + spread * spread
        total = jnp.sum(lax.rsqrt(square) * source, axis=1, keepdims=True)
        return jnp.where(lanes == n, total, check)

    check = lax.fori_loop(0, LEAF, leaf, jnp.zeros((TERMS, PTS), jnp.float32), unroll=16)
    dens = jnp.dot(up[...], check, preferred_element_type=jnp.float32, precision=EXACT_DOTS)
    turned[...] = jnp.transpose(jnp.concatenate([dens, dens], axis=0))
    even = turned[pl.ds(0, LEAF // 2, stride=2), :]
    odd = turned[pl.ds(1, LEAF // 2, stride=2), :]
    both = jnp.where(iota((LEAF // 2, PTS), 1) < TERMS, even, odd)
    for m in range(LEAF // 2):
        x, y, z = m // (CY * CZ // 2), m // (CZ // 2) % CY, m % (CZ // 2)
        wide_dens[x + 2, y + 2, z + 1] = both[m : m + 1]
    return row, counted


def points_part(pos, masked, wide_points):
    def line(x, y, carry):
        for z in range(CZ):
            n = (x * CY + y) * CZ + z
            rows = [pos[c, pl.ds(n, 1), :] for c in range(3)] + [masked[pl.ds(n, 1), :]]
            wide_points[x + 1, y + 1, z + 1] = jnp.concatenate(rows, axis=0)
        return carry

    over_plane(CX, CY, line, 0, CY)


def order_part(row, counted, order_ref):
    leaf = iota((LEAF, LEAF), 0).astype(jnp.float32)
    other = iota((LEAF, LEAF), 1).astype(jnp.float32)
    mine = counted * LEAF + leaf
    theirs = row * LEAF + other
    rank = jnp.sum(jnp.where(theirs < mine, 1.0, 0.0), axis=1, keepdims=True)
    order = jnp.sum(jnp.where(rank == other, leaf, 0.0), axis=0, keepdims=True)
    order_ref[...] = jnp.concatenate([order, row], axis=1).astype(jnp.int32)


def weights_part(inner, weights):
    upper_lanes = iota((TERMS, 2 * TERMS), 1) >= TERMS
    spread = []
    for c in range(3):
        row = inner[c : c + 1, :]
        spread.append(jnp.concatenate([row, row], axis=1) - column(row))
    squares_z = []
    for pair in range(PAIRS):
        shift = jnp.where(upper_lanes, float(pair + 1), float(pair - 3))
        squares_z.append((spread[2] - shift) * (spread[2] - shift))

    def line(n_x, n_y, carry):
        shift_x = n_x - 3
        shift_y = n_y - 3
        d_x = spread[0] - shift_x.astype(jnp.float32)
        d_y = spread[1] - shift_y.astype(jnp.float32)
        plane = d_x * d_x + d_y * d_y + SOFTEN
        close = jnp.maximum(jnp.abs(shift_x), jnp.abs(shift_y)) < 2
        for pair in range(PAIRS):
            weight = lax.rsqrt(plane + squares_z[pair])
            if pair == 0:
                weight = jnp.where(close & upper_lanes, 0.0, weight)
            if pair >= 2:
                weight = jnp.where(close & ~upper_lanes, 0.0, weight)
            high = weight.astype(jnp.bfloat16)
            low = (weight - high.astype(jnp.float32)).astype(jnp.bfloat16)
            at = (n_x * 7 + n_y) * 2
            weights[at, pair * TERMS : (pair + 1) * TERMS] = high
            weights[at + 1, pair * TERMS : (pair + 1) * TERMS] = low
        return carry

    over_plane(7, 7, line, 0, 7)


def gather_part(wide_dens, raw, grouped):
    half = iota((8, 2 * TERMS), 1) < TERMS
    blank = jnp.zeros((8, 2 * TERMS), jnp.float32)

    def line(a_x, a_y, carry):
        whole_rows = []
        for b in range(3):
            at = a_x * 18 + a_y * 3 + b
            for parent in range(8):
                cell_x = 2 * (parent // 4) + a_x
                cell_y = 2 * (parent // 2 % 2) + a_y
                raw[at, parent : parent + 1, :] = wide_dens[cell_x, cell_y, parent % 2 + b]
        for b in range(3):
            value = raw[a_x * 18 + a_y * 3 + b]
            high = rounded(value)
            whole_rows.append((high, value - high))
        for part in range(2):
            first, second, third = (member[part] for member in whole_rows)
            one, two, three = (pltpu.roll(member, TERMS, 1) for member in (first, second, third))
            tiles = [
                (jnp.where(half, 0.0, one), first),
                (jnp.where(half, one, two), second),
                (jnp.where(half, two, three), third),
                (jnp.where(half, three, 0.0), blank),
            ]
            for at, rows in enumerate(tiles):
                grouped[(a_x + 1) * 8 + a_y + 1, 4 * part + at] = jnp.concatenate(
                    rows, axis=0
                ).astype(jnp.bfloat16)
        return carry

    lax.fori_loop(
        0, 6, lambda x, held: lax.fori_loop(0, 6, lambda y, kept: line(x, y, kept), held, unroll=6), 0, unroll=6
    )


def translate_part(weights, grouped, down_ref, local):
    def product(places, parities):
        lefts = []
        rights = []
        for n_x, n_y in places:
            for lanes in range(2):
                pieces = []
                for kind in (0, 4, 2, 6):
                    for parity in parities:
                        at = (n_x + parity // 2) * 8 + n_y + parity % 2
                        pieces.append(grouped[at, kind + lanes])
                lefts.append(jnp.concatenate(pieces, axis=0))
            at = (n_x * 7 + n_y) * 2
            rights.append(jnp.concatenate([weights[at], weights[at + 1]], axis=1))
        result = jnp.dot(
            jnp.concatenate(lefts, axis=1),
            jnp.concatenate(rights, axis=0),
            preferred_element_type=jnp.float32,
        )
        for kind in range(4):
            for k, parity in enumerate(parities):
                at = (kind * len(parities) + k) * 16
                sums[kind * 4 + parity].append(result[at : at + 16])

    sums = [[] for _ in range(16)]
    inner_shifts = range(1, 6)
    product([(n_x, n_y) for n_x in inner_shifts for n_y in inner_shifts], (0, 1, 2, 3))
    product([(0, n_y) for n_y in range(7)], (2, 3))
    product([(6, n_y) for n_y in range(7)], (0, 1))
    product([(n_x, 0) for n_x in inner_shifts], (1, 3))
    product([(n_x, 6) for n_x in inner_shifts], (0, 2))
    total = jnp.concatenate([sum(rows[1:], rows[0]) for rows in sums], axis=0)
    total = total[:, : 2 * TERMS] + total[:, 2 * TERMS :]
    lower = total[:LEAF] + total[LEAF : 2 * LEAF]
    upper = total[2 * LEAF : 3 * LEAF] + total[3 * LEAF :]
    total = jnp.where(iota((LEAF, 2 * TERMS), 1) < TERMS, lower, upper)
    down = down_ref[...]
    down = jnp.concatenate([down, down], axis=1)
    down = jnp.concatenate([down, jnp.zeros_like(down)], axis=0)
    local[...] = lax.dot_general(
        total,
        down,
        (((1,), (1,)), ((), ())),
        preferred_element_type=jnp.float32,
        precision=EXACT_DOTS,
    )


def gather_body(
    pos_hbm,
    charge_hbm,
    count_hbm,
    up_hbm,
    down_hbm,
    inner_hbm,
    outer_hbm,
    wide_points,
    sources,
    targets,
    local,
    order_ref,
    wide_dens,
    pos,
    charge,
    count,
    up,
    down,
    inner,
    outer,
    masked,
    turned,
    weights,
    raw,
    grouped,
    surface,
    order_rows,
    load_sem,
    send_sem,
    recv_sem,
):
    low_bits, mid_bits, high_bits = axis_bits()
    total_bits = low_bits + mid_bits + high_bits
    device = (
        lax.axis_index("gx") * 2**mid_bits + lax.axis_index("gy")
    ) * 2**low_bits + lax.axis_index("gz")
    place = []
    extent = []
    for c in range(3):
        bits = list(range(c, total_bits, 3))
        place.append(sum(((device >> bit) & 1) * 2**rank for rank, bit in enumerate(bits)))
        extent.append(2 ** len(bits))

    steps = []
    for c in range(3):
        moves = {}
        for move in (-1, 0, 1):
            moved = place[c] + move
            spot = [0, 0, 0]
            for rank, bit in enumerate(range(c, total_bits, 3)):
                digit = (moved >> rank) & 1
                if bit < low_bits:
                    spot[2] = spot[2] + digit * 2**bit
                elif bit < low_bits + mid_bits:
                    spot[1] = spot[1] + digit * 2 ** (bit - low_bits)
                else:
                    spot[0] = spot[0] + digit * 2 ** (bit - low_bits - mid_bits)
            moves[move] = spot
        steps.append(moves)
    room = [{1: place[c] < extent[c] - 1, -1: place[c] > 0} for c in range(3)]
    inside = {}
    for side in SIDES:
        held = None
        for c in range(3):
            if side[c] != 0:
                held = room[c][side[c]] if held is None else held & room[c][side[c]]
        inside[side] = held

    def there(side):
        return inside[side]

    def coordinates(side):
        return tuple(
            sum(steps[c][side[c]][axis] for c in range(3)) + jnp.int32(0) for axis in range(3)
        )

    kinds = (
        (wide_dens, (CX, CY, CZ // 2), (2, 2, 1)),
        (wide_points, (CX, CY, CZ), (1, 1, 1)),
    )

    def regions(kind, at):
        wide, sizes, layers = kinds[kind]
        return zip(*(rim(SIDES[at][c], sizes[c], layers[c]) for c in range(3)))

    def remote(kind, at):
        wide = kinds[kind][0]
        source, target = regions(kind, at)
        return pltpu.make_async_remote_copy(
            src_ref=wide.at[source],
            dst_ref=wide.at[target],
            send_sem=send_sem.at[kind, at],
            recv_sem=recv_sem.at[kind, at],
            device_id=coordinates(SIDES[at]),
            device_id_type=pl.DeviceIdType.MESH,
        )

    loads = [
        pltpu.make_async_copy(source, target, load_sem.at[at])
        for at, (source, target) in enumerate(
            (
                (pos_hbm, pos),
                (charge_hbm, charge),
                (count_hbm, count),
                (outer_hbm, outer),
                (up_hbm, up),
                (inner_hbm, inner),
                (down_hbm, down),
            )
        )
    ]
    for load in loads:
        load.start()
    barrier = pltpu.get_barrier_semaphore()
    met = jnp.int32(0)
    order = sorted(range(len(SIDES)), key=lambda at: -sum(map(abs, SIDES[at])))
    for at in order:
        met = met + jnp.where(there(SIDES[at]), 1, 0)

        @pl.when(there(SIDES[at]))
        def _(at=at):
            pl.semaphore_signal(
                barrier,
                inc=1,
                device_id=coordinates(SIDES[at]),
                device_id_type=pl.DeviceIdType.MESH,
            )

    clear_part(grouped, surface)
    for load in loads:
        load.wait()
    surface[0:3, 0:TERMS] = outer[...]
    row, counted = upward_part(
        pos, charge, count, up, outer, masked, turned, wide_points, wide_dens, order_ref
    )
    pl.semaphore_wait(barrier, met)

    def send(kind):
        for at in order:

            @pl.when(there(SIDES[at]))
            def _(at=at):
                remote(kind, at).start()

    def sent(kind):
        for at in order:

            @pl.when(there(SIDES[at]))
            def _(at=at):
                remote(kind, at).wait_send()

    def finish(kind):
        for at in order:

            @pl.when(there(tuple(-c for c in SIDES[at])))
            def _(at=at):
                remote(kind, at).wait_recv()

    def blank(kind):
        for at in order:

            @pl.when(~there(tuple(-c for c in SIDES[at])))
            def _(at=at):
                wide = kinds[kind][0]
                _, target = regions(kind, at)
                shape = tuple(piece.size for piece in target) + wide.shape[3:]
                wide[target] = jnp.zeros(shape, jnp.float32)

    send(0)
    points_part(pos, masked, wide_points)
    send(1)
    order_part(row, counted, order_rows)
    ordering = pltpu.make_async_copy(order_rows, order_ref, load_sem.at[7])
    ordering.start()
    blank(0)
    blank(1)
    weights_part(inner, weights)

    def source(e_x, e_y, e_z, other):
        base = (e_x * (CY + 2) + e_y) * (CZ + 2)
        made = source_features(
            [wide_points[e_x, e_y, at] for at in (e_z, other)],
            [(middle(e_x), middle(e_y), middle(at)) for at in (e_z, other)],
        )
        for at, features in zip((e_z, other), made):
            sources[base + at] = features

    def prepare_own(x, y, carry):
        for z in range(0, CZ, 2):
            source(x + 1, y + 1, z + 1, z + 2)
            n = (x * CY + y) * CZ + z
            spots = [(middle(x + 1), middle(y + 1), middle(z + k + 1)) for k in range(2)]
            for k, features in enumerate(source_features([surface[...]] * 2, spots)):
                sources[EXT + n + k] = features
            for k in range(2):
                points = wide_points[x + 1, y + 1, z + k + 1]
                targets[n + k] = target_features(points, *spots[k])
        return carry

    over_plane(CX, CY, prepare_own, 0, CY)
    ordering.wait()
    sent(0)
    finish(0)
    gather_part(wide_dens, raw, grouped)
    translate_part(weights, grouped, down, local)
    sent(1)
    finish(1)

    def prepare_ends(y, carry):
        for e_x in (0, CX + 1):
            for e_z in range(0, CZ + 2, 2):
                source(e_x, y, e_z, e_z + 1)
        return carry

    def prepare_sides(x, carry):
        for e_y in (0, CY + 1):
            for e_z in range(0, CZ + 2, 2):
                source(x, e_y, e_z, e_z + 1)
        for e_y in range(1, CY + 1):
            source(x, e_y, 0, CZ + 1)
        return carry

    lax.fori_loop(0, CY + 2, prepare_ends, 0, unroll=3)
    lax.fori_loop(1, CX + 1, prepare_sides, 0, unroll=2)


def near_body(order_ref, points_ref, sources, targets, local, out_ref, totals):
    lane = iota((1, PTS), 1)
    square_eye = iota((PTS, PTS), 0) == iota((PTS, PTS), 1)

    def rows(n, size):
        x, y, z = n >> 4, (n >> 2) & 3, n & 3
        base = ext_index(x, y, z)
        parity = (x & 1) * 4 + (y & 1) * 2 + (z & 1)
        parent = (x >> 1) * 4 + (y >> 1) * 2 + (z >> 1)
        blocks = []
        for s_x in range(-1, 2):
            for s_y in range(-1, 2):
                for s_z in range(-1, 2):
                    blocks.append(base + s_x * ((CY + 2) * (CZ + 2)) + s_y * (CZ + 2) + s_z)
        left = targets[n, 0:size, :]
        eye = iota((size, PTS), 0) == iota((size, PTS), 1)
        total = jnp.zeros((size, PTS), jnp.float32)
        for at in range(0, 28, 2):
            right = []
            charge = []
            for b in (at, at + 1):
                if b < 27:
                    right.append(sources[blocks[b]])
                    charge.append(points_ref[blocks[b], 3:4, :])
                else:
                    right.append(sources[EXT + n])
                    charge.append(local[pl.ds(parity * 8 + parent, 1), :])
            square = jnp.dot(
                left, jnp.concatenate(right, axis=1), preferred_element_type=jnp.float32
            )
            weight = lax.rsqrt(square)
            for k, b in enumerate((at, at + 1)):
                part = weight[:, k * PTS : (k + 1) * PTS]
                if b == 13:
                    part = jnp.where(eye, 0.0, part)
                total = total + part * charge[k]
        return total

    def finish(g):
        for k in range(LINE):
            n = order_ref[0, g * LINE + k]
            sums = jnp.sum(totals[k], axis=1, keepdims=True)
            flat = jnp.sum(jnp.where(square_eye, sums, 0.0), axis=0, keepdims=True)
            out_ref[pl.ds(n, 1), :] = jnp.where(lane < order_ref[0, LEAF + n], flat, 0.0)

    def leaf_group(g, carry):
        def steps_of(k):
            return lax.div(order_ref[0, LEAF + order_ref[0, g * LINE + k]] + STEP - 1, STEP)

        most = steps_of(LINE - 1)
        alike = steps_of(LINE // 2 - 1) == most

        def together(lower, upper):
            finish(jnp.maximum(g - 1, 0))
            for k in range(LINE):
                size = lower if k < LINE // 2 else upper
                totals[k, 0:size, :] = rows(order_ref[0, g * LINE + k], size)

        def among(low, high):
            if high - low == 1:
                size = STEP * high
                if low == 0:
                    together(size, size)
                else:
                    pl.when(alike)(partial(together, size, size))
                    pl.when(~alike)(partial(together, size - STEP, size))
                return
            mid = (low + high) // 2
            pl.when(most <= mid)(partial(among, low, mid))
            pl.when(most > mid)(partial(among, mid, high))

        among(0, PTS // STEP)
        return carry

    lax.fori_loop(0, LEAF // LINE, leaf_group, 0)
    finish(LEAF // LINE - 1)


def gather_all(positions, charges, counts, up_inverse, down_inverse, inner_surface, outer_surface):
    wide = (CX + 2, CY + 2, CZ + 2, 4, PTS)
    return pl.pallas_call(
        gather_body,
        out_shape=(
            pltpu.VMEM(wide, jnp.float32),
            pltpu.VMEM((EXT + LEAF, FEATS, PTS), jnp.bfloat16),
            pltpu.VMEM((LEAF, PTS, FEATS), jnp.bfloat16),
            pltpu.VMEM((LEAF, 2 * TERMS), jnp.float32),
            pltpu.SMEM((1, 2 * LEAF), jnp.int32),
        ),
        in_specs=[anywhere()] * 7,
        out_specs=(whole(),) * 4 + (scalars(),),
        scratch_shapes=[
            pltpu.VMEM((CX + 4, CY + 4, CZ // 2 + 2, 1, 2 * TERMS), jnp.float32),
            pltpu.VMEM((3, LEAF, PTS), jnp.float32),
            pltpu.VMEM((LEAF, PTS), jnp.float32),
            pltpu.VMEM((1, LEAF), jnp.int32),
            pltpu.VMEM((TERMS, TERMS), jnp.float32),
            pltpu.VMEM((TERMS, TERMS), jnp.float32),
            pltpu.VMEM((3, TERMS), jnp.float32),
            pltpu.VMEM((3, TERMS), jnp.float32),
            pltpu.VMEM((LEAF, PTS), jnp.float32),
            pltpu.VMEM((PTS, 2 * TERMS), jnp.float32),
            pltpu.VMEM((98, PAIRS * TERMS, 2 * TERMS), jnp.bfloat16),
            pltpu.VMEM((108, 8, 2 * TERMS), jnp.float32),
            pltpu.VMEM((64, 8, 16, 2 * TERMS), jnp.bfloat16),
            pltpu.VMEM((4, PTS), jnp.float32),
            pltpu.VMEM((1, 2 * LEAF), jnp.int32),
            pltpu.SemaphoreType.DMA((8,)),
            pltpu.SemaphoreType.DMA((2, len(SIDES))),
            pltpu.SemaphoreType.DMA((2, len(SIDES))),
        ],
        compiler_params=pltpu.CompilerParams(
            collective_id=0, has_side_effects=True, vmem_limit_bytes=32 * 2**20
        ),
        name="gather",
    )(positions, charges, counts, up_inverse, down_inverse, inner_surface, outer_surface)


def potentials(order, points, sources, targets, local):
    return pl.pallas_call(
        near_body,
        out_shape=jax.ShapeDtypeStruct((LEAF, PTS), jnp.float32),
        in_specs=[scalars()] + [whole()] * 4,
        out_specs=whole(),
        scratch_shapes=[pltpu.VMEM((LINE, PTS, PTS), jnp.float32)],
        compiler_params=pltpu.CompilerParams(vmem_limit_bytes=32 * 2**20),
        name="potentials",
    )(order, points, sources, targets, local)


def per_device(positions, charges, counts, up_inverse, down_inverse, inner_surface, outer_surface):
    arguments = (
        jnp.transpose(positions, (1, 0, 2)),
        charges,
        counts.reshape(1, LEAF),
        up_inverse,
        down_inverse,
        inner_surface,
        outer_surface,
    )
    points, sources, targets, local, order = gather_all(
        *(pltpu.with_memory_space_constraint(member, pltpu.HBM) for member in arguments)
    )
    return potentials(order, points.reshape(EXT, 4, PTS), sources, targets, local)


def solution(mesh):
    in_specs = (
        P(("gx", "gy", "gz"), None, None),
        P(("gx", "gy", "gz"), None),
        P(("gx", "gy", "gz")),
        P(),
        P(),
        P(),
        P(),
    )
    out_specs = P(("gx", "gy", "gz"), None)
    return jax.shard_map(
        per_device, mesh=mesh, in_specs=in_specs, out_specs=out_specs, check_vma=False
    )
```

```python
from functools import partial

import jax
import jax.numpy as jnp
from jax import lax
from jax.experimental import pallas as pl
from jax.experimental.pallas import tpu as pltpu
from jax.sharding import PartitionSpec as P

CX = 4
CY = 4
CZ = 4
PTS = 128
TERMS = 64
LEAF = CX * CY * CZ
EXT = (CX + 2) * (CY + 2) * (CZ + 2)
FEATS = 32
LINE = 8
PAIRS = 4
STEP = 16


SOFTEN = 0.0025
EXACT_DOTS = lax.Precision.HIGHEST


def iota(shape, dimension):
    return lax.broadcasted_iota(jnp.int32, shape, dimension)


def column(row):
    size = row.shape[1]
    eye = iota((size, size), 0) == iota((size, size), 1)
    return jnp.sum(jnp.where(eye, row, 0.0), axis=1, keepdims=True)


def over_plane(size_x, size_y, body, start, unroll=1):
    def line(x, carry):
        return lax.fori_loop(0, size_y, lambda y, held: body(x, y, held), carry, unroll=unroll)

    return lax.fori_loop(0, size_x, line, start)


def rounded(value):
    return value.astype(jnp.bfloat16).astype(jnp.float32)


def three_parts(value):
    high = rounded(value)
    middle = rounded(value - high)
    low = rounded(value - high - middle)
    return high, middle, low


def squares_of(points, shift_x, shift_y, shift_z, extra):
    row = iota((8, PTS), 0) % 4
    twice = jnp.concatenate([points, points], axis=0)
    place = twice + jnp.where(row == 0, shift_x, jnp.where(row == 1, shift_y, shift_z))
    square = place * place
    norm = square[0:1] + square[1:2] + square[2:3] + extra
    return jnp.where(row == 3, norm, place), row == 3, iota((8, PTS), 0) < 4


def source_features(points, spots):
    row = iota((8, PTS), 0)
    last, first = row % 4 == 3, row < 4
    both = jnp.concatenate(points, axis=0)
    shift = jnp.where(first, spots[0][2], spots[1][2])
    shift = jnp.where(row % 4 == 0, jnp.where(first, spots[0][0], spots[1][0]), shift)
    shift = jnp.where(row % 4 == 1, jnp.where(first, spots[0][1], spots[1][1]), shift)
    place = both + shift
    square = place * place
    norm = pltpu.roll(square, 1, 0) + pltpu.roll(square, 2, 0) + pltpu.roll(square, 3, 0)
    high, middle, low = three_parts(jnp.where(last, norm, -2.0 * place))
    high_one = jnp.where(last, 1.0, high)
    middle_one = jnp.where(last, 1.0, middle)
    pairs = ((high, middle), (low, high_one), (high_one, middle_one))
    blank = jnp.zeros((8, PTS), jnp.float32)
    lower = [jnp.where(first, one, pltpu.roll(two, 4, 0)) for one, two in pairs]
    upper = [jnp.where(first, pltpu.roll(one, 4, 0), two) for one, two in pairs]
    return [
        jnp.concatenate(rows + [blank], axis=0).astype(jnp.bfloat16) for rows in (lower, upper)
    ]


def target_features(points, shift_x, shift_y, shift_z):
    value, last, first = squares_of(points, shift_x, shift_y, shift_z, SOFTEN)
    high, middle, low = three_parts(value)
    high_one = jnp.where(last, 1.0, high)
    rows = [
        high_one,
        jnp.where(first, high_one, jnp.where(last, high, middle)),
        jnp.where(first, jnp.where(last, middle, low), jnp.where(last, low, middle)),
        jnp.zeros((8, PTS), jnp.float32),
    ]
    return jnp.transpose(jnp.concatenate(rows, axis=0)).astype(jnp.bfloat16)


def whole():
    return pl.BlockSpec(memory_space=pltpu.VMEM)


def scalars():
    return pl.BlockSpec(memory_space=pltpu.SMEM)


def anywhere():
    return pl.BlockSpec(memory_space=pl.ANY)


def axis_bits():
    low_bits = lax.axis_size("gz").bit_length() - 1
    mid_bits = lax.axis_size("gy").bit_length() - 1
    high_bits = lax.axis_size("gx").bit_length() - 1
    return (low_bits, mid_bits, high_bits)


SIDES = [
    (x, y, z)
    for x in (-1, 0, 1)
    for y in (-1, 0, 1)
    for z in (-1, 0, 1)
    if (x, y, z) != (0, 0, 0)
]


def rim(side, size, layers):
    if side > 0:
        return pl.ds(size, layers), pl.ds(0, layers)
    if side < 0:
        return pl.ds(layers, layers), pl.ds(size + layers, layers)
    return pl.ds(layers, size), pl.ds(layers, size)


def middle(cell):
    if isinstance(cell, int):
        return jnp.float32(cell) - (CX // 2 + 1)
    return cell.astype(jnp.float32) - (CX // 2 + 1)


def ext_index(x, y, z):
    return ((x + 1) * (CY + 2) + y + 1) * (CZ + 2) + z + 1


def clear_part(grouped, surface):
    def one(n, carry):
        grouped[n] = jnp.zeros((8, 16, 2 * TERMS), jnp.bfloat16)
        return carry

    lax.fori_loop(0, 64, one, 0)
    surface[...] = jnp.zeros((4, PTS), jnp.float32)


def upward_part(pos, charge, count, up, outer, masked, turned, wide_points, wide_dens, order_ref):
    row = count[...].astype(jnp.float32)
    counted = column(row)
    masked[...] = jnp.where(
        iota((LEAF, PTS), 1).astype(jnp.float32) < counted, charge[...], 0.0
    )
    spots = [jnp.broadcast_to(column(outer[c : c + 1, :]), (TERMS, PTS)) for c in range(3)]
    lanes = iota((TERMS, PTS), 1)

    def leaf(n, check):
        source = masked[pl.ds(n, 1), :]
        square = jnp.full((TERMS, PTS), SOFTEN, jnp.float32)
        for c in range(3):
            spread = spots[c] - pos[c, pl.ds(n, 1), :]
            square = square + spread * spread
        total = jnp.sum(lax.rsqrt(square) * source, axis=1, keepdims=True)
        return jnp.where(lanes == n, total, check)

    check = lax.fori_loop(0, LEAF, leaf, jnp.zeros((TERMS, PTS), jnp.float32), unroll=16)
    dens = jnp.dot(up[...], check, preferred_element_type=jnp.float32, precision=EXACT_DOTS)
    turned[...] = jnp.transpose(jnp.concatenate([dens, dens], axis=0))
    even = turned[pl.ds(0, LEAF // 2, stride=2), :]
    odd = turned[pl.ds(1, LEAF // 2, stride=2), :]
    both = jnp.where(iota((LEAF // 2, PTS), 1) < TERMS, even, odd)
    for m in range(LEAF // 2):
        x, y, z = m // (CY * CZ // 2), m // (CZ // 2) % CY, m % (CZ // 2)
        wide_dens[x + 2, y + 2, z + 1] = both[m : m + 1]
    return row, counted


def points_part(pos, masked, wide_points):
    def line(x, y, carry):
        for z in range(CZ):
            n = (x * CY + y) * CZ + z
            rows = [pos[c, pl.ds(n, 1), :] for c in range(3)] + [masked[pl.ds(n, 1), :]]
            wide_points[x + 1, y + 1, z + 1] = jnp.concatenate(rows, axis=0)
        return carry

    over_plane(CX, CY, line, 0, CY)


def order_part(row, counted, order_ref):
    leaf = iota((LEAF, LEAF), 0).astype(jnp.float32)
    other = iota((LEAF, LEAF), 1).astype(jnp.float32)
    mine = counted * LEAF + leaf
    theirs = row * LEAF + other
    rank = jnp.sum(jnp.where(theirs < mine, 1.0, 0.0), axis=1, keepdims=True)
    order = jnp.sum(jnp.where(rank == other, leaf, 0.0), axis=0, keepdims=True)
    order_ref[...] = jnp.concatenate([order, row], axis=1).astype(jnp.int32)


def weights_part(inner, weights):
    upper_lanes = iota((TERMS, 2 * TERMS), 1) >= TERMS
    spread = []
    for c in range(3):
        row = inner[c : c + 1, :]
        spread.append(jnp.concatenate([row, row], axis=1) - column(row))
    squares_z = []
    for pair in range(PAIRS):
        shift = jnp.where(upper_lanes, float(pair + 1), float(pair - 3))
        squares_z.append((spread[2] - shift) * (spread[2] - shift))

    def line(n_x, n_y, carry):
        shift_x = n_x - 3
        shift_y = n_y - 3
        d_x = spread[0] - shift_x.astype(jnp.float32)
        d_y = spread[1] - shift_y.astype(jnp.float32)
        plane = d_x * d_x + d_y * d_y + SOFTEN
        close = jnp.maximum(jnp.abs(shift_x), jnp.abs(shift_y)) < 2
        for pair in range(PAIRS):
            weight = lax.rsqrt(plane + squares_z[pair])
            if pair == 0:
                weight = jnp.where(close & upper_lanes, 0.0, weight)
            if pair >= 2:
                weight = jnp.where(close & ~upper_lanes, 0.0, weight)
            high = weight.astype(jnp.bfloat16)
            low = (weight - high.astype(jnp.float32)).astype(jnp.bfloat16)
            at = (n_x * 7 + n_y) * 2
            weights[at, pair * TERMS : (pair + 1) * TERMS] = high
            weights[at + 1, pair * TERMS : (pair + 1) * TERMS] = low
        return carry

    over_plane(7, 7, line, 0, 7)


def gather_part(wide_dens, raw, grouped):
    half = iota((8, 2 * TERMS), 1) < TERMS
    blank = jnp.zeros((8, 2 * TERMS), jnp.float32)

    def line(a_x, a_y, carry):
        whole_rows = []
        for b in range(3):
            at = a_x * 18 + a_y * 3 + b
            for parent in range(8):
                cell_x = 2 * (parent // 4) + a_x
                cell_y = 2 * (parent // 2 % 2) + a_y
                raw[at, parent : parent + 1, :] = wide_dens[cell_x, cell_y, parent % 2 + b]
        for b in range(3):
            value = raw[a_x * 18 + a_y * 3 + b]
            high = rounded(value)
            whole_rows.append((high, value - high))
        for part in range(2):
            first, second, third = (member[part] for member in whole_rows)
            one, two, three = (pltpu.roll(member, TERMS, 1) for member in (first, second, third))
            tiles = [
                (jnp.where(half, 0.0, one), first),
                (jnp.where(half, one, two), second),
                (jnp.where(half, two, three), third),
                (jnp.where(half, three, 0.0), blank),
            ]
            for at, rows in enumerate(tiles):
                grouped[(a_x + 1) * 8 + a_y + 1, 4 * part + at] = jnp.concatenate(
                    rows, axis=0
                ).astype(jnp.bfloat16)
        return carry

    lax.fori_loop(
        0, 6, lambda x, held: lax.fori_loop(0, 6, lambda y, kept: line(x, y, kept), held, unroll=6), 0, unroll=6
    )


def product(weights, grouped, sums, places, parities):
    lefts = []
    rights = []
    for n_x, n_y in places:
        for lanes in range(2):
            pieces = []
            for kind in (0, 4, 2, 6):
                for parity in parities:
                    at = (n_x + parity // 2) * 8 + n_y + parity % 2
                    pieces.append(grouped[at, kind + lanes])
            lefts.append(jnp.concatenate(pieces, axis=0))
        at = (n_x * 7 + n_y) * 2
        rights.append(jnp.concatenate([weights[at], weights[at + 1]], axis=1))
    result = jnp.dot(
        jnp.concatenate(lefts, axis=1),
        jnp.concatenate(rights, axis=0),
        preferred_element_type=jnp.float32,
    )
    for kind in range(4):
        for k, parity in enumerate(parities):
            at = (kind * len(parities) + k) * 16
            sums[kind * 4 + parity].append(result[at : at + 16])


def translate_inner(weights, grouped):
    inner_shifts = range(1, 6)
    sums = [[] for _ in range(16)]
    places = [(n_x, n_y) for n_x in inner_shifts for n_y in inner_shifts]
    product(weights, grouped, sums, places, (0, 1, 2, 3))
    return sums


def translate_outer(sums, weights, grouped, down_ref, local):
    inner_shifts = range(1, 6)
    product(weights, grouped, sums, [(0, n_y) for n_y in range(7)], (2, 3))
    product(weights, grouped, sums, [(6, n_y) for n_y in range(7)], (0, 1))
    product(weights, grouped, sums, [(n_x, 0) for n_x in inner_shifts], (1, 3))
    product(weights, grouped, sums, [(n_x, 6) for n_x in inner_shifts], (0, 2))
    total = jnp.concatenate([sum(rows[1:], rows[0]) for rows in sums], axis=0)
    total = total[:, : 2 * TERMS] + total[:, 2 * TERMS :]
    lower = total[:LEAF] + total[LEAF : 2 * LEAF]
    upper = total[2 * LEAF : 3 * LEAF] + total[3 * LEAF :]
    total = jnp.where(iota((LEAF, 2 * TERMS), 1) < TERMS, lower, upper)
    down = down_ref[...]
    down = jnp.concatenate([down, down], axis=1)
    down = jnp.concatenate([down, jnp.zeros_like(down)], axis=0)
    local[...] = lax.dot_general(
        total,
        down,
        (((1,), (1,)), ((), ())),
        preferred_element_type=jnp.float32,
        precision=EXACT_DOTS,
    )


def gather_body(
    pos_hbm,
    charge_hbm,
    count_hbm,
    up_hbm,
    down_hbm,
    inner_hbm,
    outer_hbm,
    wide_points,
    sources,
    targets,
    local,
    order_ref,
    wide_dens,
    pos,
    charge,
    count,
    up,
    down,
    inner,
    outer,
    masked,
    turned,
    weights,
    raw,
    grouped,
    surface,
    order_rows,
    load_sem,
    send_sem,
    recv_sem,
):
    low_bits, mid_bits, high_bits = axis_bits()
    total_bits = low_bits + mid_bits + high_bits
    device = (
        lax.axis_index("gx") * 2**mid_bits + lax.axis_index("gy")
    ) * 2**low_bits + lax.axis_index("gz")
    place = []
    extent = []
    for c in range(3):
        bits = list(range(c, total_bits, 3))
        place.append(sum(((device >> bit) & 1) * 2**rank for rank, bit in enumerate(bits)))
        extent.append(2 ** len(bits))

    steps = []
    for c in range(3):
        moves = {}
        for move in (-1, 0, 1):
            moved = place[c] + move
            spot = [0, 0, 0]
            for rank, bit in enumerate(range(c, total_bits, 3)):
                digit = (moved >> rank) & 1
                if bit < low_bits:
                    spot[2] = spot[2] + digit * 2**bit
                elif bit < low_bits + mid_bits:
                    spot[1] = spot[1] + digit * 2 ** (bit - low_bits)
                else:
                    spot[0] = spot[0] + digit * 2 ** (bit - low_bits - mid_bits)
            moves[move] = spot
        steps.append(moves)
    room = [{1: place[c] < extent[c] - 1, -1: place[c] > 0} for c in range(3)]
    inside = {}
    for side in SIDES:
        held = None
        for c in range(3):
            if side[c] != 0:
                held = room[c][side[c]] if held is None else held & room[c][side[c]]
        inside[side] = held

    def there(side):
        return inside[side]

    def coordinates(side):
        return tuple(
            sum(steps[c][side[c]][axis] for c in range(3)) + jnp.int32(0) for axis in range(3)
        )

    kinds = (
        (wide_dens, (CX, CY, CZ // 2), (2, 2, 1)),
        (wide_points, (CX, CY, CZ), (1, 1, 1)),
    )

    def regions(kind, at):
        wide, sizes, layers = kinds[kind]
        return zip(*(rim(SIDES[at][c], sizes[c], layers[c]) for c in range(3)))

    def remote(kind, at):
        wide = kinds[kind][0]
        source, target = regions(kind, at)
        return pltpu.make_async_remote_copy(
            src_ref=wide.at[source],
            dst_ref=wide.at[target],
            send_sem=send_sem.at[kind, at],
            recv_sem=recv_sem.at[kind, at],
            device_id=coordinates(SIDES[at]),
            device_id_type=pl.DeviceIdType.MESH,
        )

    loads = [
        pltpu.make_async_copy(source, target, load_sem.at[at])
        for at, (source, target) in enumerate(
            (
                (pos_hbm, pos),
                (charge_hbm, charge),
                (count_hbm, count),
                (outer_hbm, outer),
                (up_hbm, up),
                (inner_hbm, inner),
                (down_hbm, down),
            )
        )
    ]
    for load in loads:
        load.start()
    barrier = pltpu.get_barrier_semaphore()
    met = jnp.int32(0)
    order = sorted(range(len(SIDES)), key=lambda at: -sum(map(abs, SIDES[at])))
    for at in order:
        met = met + jnp.where(there(SIDES[at]), 1, 0)

        @pl.when(there(SIDES[at]))
        def _(at=at):
            pl.semaphore_signal(
                barrier,
                inc=1,
                device_id=coordinates(SIDES[at]),
                device_id_type=pl.DeviceIdType.MESH,
            )

    clear_part(grouped, surface)
    for load in loads:
        load.wait()
    surface[0:3, 0:TERMS] = outer[...]
    row, counted = upward_part(
        pos, charge, count, up, outer, masked, turned, wide_points, wide_dens, order_ref
    )
    pl.semaphore_wait(barrier, met)

    def send(kind):
        for at in order:

            @pl.when(there(SIDES[at]))
            def _(at=at):
                remote(kind, at).start()

    def sent(kind):
        for at in order:

            @pl.when(there(SIDES[at]))
            def _(at=at):
                remote(kind, at).wait_send()

    def finish(kind):
        for at in order:

            @pl.when(there(tuple(-c for c in SIDES[at])))
            def _(at=at):
                remote(kind, at).wait_recv()

    def blank(kind):
        for at in order:

            @pl.when(~there(tuple(-c for c in SIDES[at])))
            def _(at=at):
                wide = kinds[kind][0]
                _, target = regions(kind, at)
                shape = tuple(piece.size for piece in target) + wide.shape[3:]
                wide[target] = jnp.zeros(shape, jnp.float32)

    send(0)
    points_part(pos, masked, wide_points)
    send(1)
    order_part(row, counted, order_rows)
    ordering = pltpu.make_async_copy(order_rows, order_ref, load_sem.at[7])
    ordering.start()
    blank(0)
    blank(1)
    weights_part(inner, weights)

    def source(e_x, e_y, e_z, other):
        base = (e_x * (CY + 2) + e_y) * (CZ + 2)
        made = source_features(
            [wide_points[e_x, e_y, at] for at in (e_z, other)],
            [(middle(e_x), middle(e_y), middle(at)) for at in (e_z, other)],
        )
        for at, features in zip((e_z, other), made):
            sources[base + at] = features

    def prepare_own(x, y, carry):
        for z in range(0, CZ, 2):
            source(x + 1, y + 1, z + 1, z + 2)
            n = (x * CY + y) * CZ + z
            spots = [(middle(x + 1), middle(y + 1), middle(z + k + 1)) for k in range(2)]
            for k, features in enumerate(source_features([surface[...]] * 2, spots)):
                sources[EXT + n + k] = features
            for k in range(2):
                points = wide_points[x + 1, y + 1, z + k + 1]
                targets[n + k] = target_features(points, *spots[k])
        return carry

    over_plane(CX, CY, prepare_own, 0, CY)
    ordering.wait()
    sent(0)
    finish(0)
    gather_part(wide_dens, raw, grouped)
    sums = translate_inner(weights, grouped)
    sent(1)
    finish(1)

    def prepare_ends(y, carry):
        for e_x in (0, CX + 1):
            for e_z in range(0, CZ + 2, 2):
                source(e_x, y, e_z, e_z + 1)
        return carry

    def prepare_sides(x, carry):
        for e_y in (0, CY + 1):
            for e_z in range(0, CZ + 2, 2):
                source(x, e_y, e_z, e_z + 1)
        for e_y in range(1, CY + 1):
            source(x, e_y, 0, CZ + 1)
        return carry

    lax.fori_loop(0, CY + 2, prepare_ends, 0, unroll=CY + 2)
    lax.fori_loop(1, CX + 1, prepare_sides, 0, unroll=CX)
    translate_outer(sums, weights, grouped, down, local)


def near_body(order_ref, points_ref, sources, targets, local, out_ref, totals):
    lane = iota((1, PTS), 1)
    square_eye = iota((PTS, PTS), 0) == iota((PTS, PTS), 1)

    def rows(n, size):
        x, y, z = n >> 4, (n >> 2) & 3, n & 3
        base = ext_index(x, y, z)
        parity = (x & 1) * 4 + (y & 1) * 2 + (z & 1)
        parent = (x >> 1) * 4 + (y >> 1) * 2 + (z >> 1)
        blocks = []
        for s_x in range(-1, 2):
            for s_y in range(-1, 2):
                for s_z in range(-1, 2):
                    blocks.append(base + s_x * ((CY + 2) * (CZ + 2)) + s_y * (CZ + 2) + s_z)
        left = targets[n, 0:size, :]
        eye = iota((size, PTS), 0) == iota((size, PTS), 1)
        total = jnp.zeros((size, PTS), jnp.float32)
        for at in range(0, 28, 2):
            right = []
            charge = []
            for b in (at, at + 1):
                if b < 27:
                    right.append(sources[blocks[b]])
                    charge.append(points_ref[blocks[b], 3:4, :])
                else:
                    right.append(sources[EXT + n])
                    charge.append(local[pl.ds(parity * 8 + parent, 1), :])
            square = jnp.dot(
                left, jnp.concatenate(right, axis=1), preferred_element_type=jnp.float32
            )
            weight = lax.rsqrt(square)
            for k, b in enumerate((at, at + 1)):
                part = weight[:, k * PTS : (k + 1) * PTS]
                if b == 13:
                    part = jnp.where(eye, 0.0, part)
                total = total + part * charge[k]
        return total

    def finish(g):
        for k in range(LINE):
            n = order_ref[0, g * LINE + k]
            sums = jnp.sum(totals[k], axis=1, keepdims=True)
            flat = jnp.sum(jnp.where(square_eye, sums, 0.0), axis=0, keepdims=True)
            out_ref[pl.ds(n, 1), :] = jnp.where(lane < order_ref[0, LEAF + n], flat, 0.0)

    def leaf_group(g, carry):
        def steps_of(k):
            return lax.div(order_ref[0, LEAF + order_ref[0, g * LINE + k]] + STEP - 1, STEP)

        most = steps_of(LINE - 1)
        alike = steps_of(LINE // 2 - 1) == most

        def together(lower, upper):
            finish(jnp.maximum(g - 1, 0))
            for k in range(LINE):
                size = lower if k < LINE // 2 else upper
                totals[k, 0:size, :] = rows(order_ref[0, g * LINE + k], size)

        def among(low, high):
            if high - low == 1:
                size = STEP * high
                if low == 0:
                    together(size, size)
                else:
                    pl.when(alike)(partial(together, size, size))
                    pl.when(~alike)(partial(together, size - STEP, size))
                return
            mid = (low + high) // 2
            pl.when(most <= mid)(partial(among, low, mid))
            pl.when(most > mid)(partial(among, mid, high))

        among(0, PTS // STEP)
        return carry

    lax.fori_loop(0, LEAF // LINE, leaf_group, 0)
    finish(LEAF // LINE - 1)


def gather_all(positions, charges, counts, up_inverse, down_inverse, inner_surface, outer_surface):
    wide = (CX + 2, CY + 2, CZ + 2, 4, PTS)
    return pl.pallas_call(
        gather_body,
        out_shape=(
            pltpu.VMEM(wide, jnp.float32),
            pltpu.VMEM((EXT + LEAF, FEATS, PTS), jnp.bfloat16),
            pltpu.VMEM((LEAF, PTS, FEATS), jnp.bfloat16),
            pltpu.VMEM((LEAF, 2 * TERMS), jnp.float32),
            pltpu.SMEM((1, 2 * LEAF), jnp.int32),
        ),
        in_specs=[anywhere()] * 7,
        out_specs=(whole(),) * 4 + (scalars(),),
        scratch_shapes=[
            pltpu.VMEM((CX + 4, CY + 4, CZ // 2 + 2, 1, 2 * TERMS), jnp.float32),
            pltpu.VMEM((3, LEAF, PTS), jnp.float32),
            pltpu.VMEM((LEAF, PTS), jnp.float32),
            pltpu.VMEM((1, LEAF), jnp.int32),
            pltpu.VMEM((TERMS, TERMS), jnp.float32),
            pltpu.VMEM((TERMS, TERMS), jnp.float32),
            pltpu.VMEM((3, TERMS), jnp.float32),
            pltpu.VMEM((3, TERMS), jnp.float32),
            pltpu.VMEM((LEAF, PTS), jnp.float32),
            pltpu.VMEM((PTS, 2 * TERMS), jnp.float32),
            pltpu.VMEM((98, PAIRS * TERMS, 2 * TERMS), jnp.bfloat16),
            pltpu.VMEM((108, 8, 2 * TERMS), jnp.float32),
            pltpu.VMEM((64, 8, 16, 2 * TERMS), jnp.bfloat16),
            pltpu.VMEM((4, PTS), jnp.float32),
            pltpu.VMEM((1, 2 * LEAF), jnp.int32),
            pltpu.SemaphoreType.DMA((8,)),
            pltpu.SemaphoreType.DMA((2, len(SIDES))),
            pltpu.SemaphoreType.DMA((2, len(SIDES))),
        ],
        compiler_params=pltpu.CompilerParams(
            collective_id=0, has_side_effects=True, vmem_limit_bytes=32 * 2**20
        ),
        name="gather",
    )(positions, charges, counts, up_inverse, down_inverse, inner_surface, outer_surface)


def potentials(order, points, sources, targets, local):
    return pl.pallas_call(
        near_body,
        out_shape=jax.ShapeDtypeStruct((LEAF, PTS), jnp.float32),
        in_specs=[scalars()] + [whole()] * 4,
        out_specs=whole(),
        scratch_shapes=[pltpu.VMEM((LINE, PTS, PTS), jnp.float32)],
        compiler_params=pltpu.CompilerParams(vmem_limit_bytes=32 * 2**20),
        name="potentials",
    )(order, points, sources, targets, local)


def per_device(positions, charges, counts, up_inverse, down_inverse, inner_surface, outer_surface):
    arguments = (
        jnp.transpose(positions, (1, 0, 2)),
        charges,
        counts.reshape(1, LEAF),
        up_inverse,
        down_inverse,
        inner_surface,
        outer_surface,
    )
    points, sources, targets, local, order = gather_all(
        *(pltpu.with_memory_space_constraint(member, pltpu.HBM) for member in arguments)
    )
    return potentials(order, points.reshape(EXT, 4, PTS), sources, targets, local)


def solution(mesh):
    in_specs = (
        P(("gx", "gy", "gz"), None, None),
        P(("gx", "gy", "gz"), None),
        P(("gx", "gy", "gz")),
        P(),
        P(),
        P(),
        P(),
    )
    out_specs = P(("gx", "gy", "gz"), None)
    return jax.shard_map(
        per_device, mesh=mesh, in_specs=in_specs, out_specs=out_specs, check_vma=False
    )
```
